256 devices in a mesh: prow: 16 (over x, y), pcol: 16 (over z, core).
Axes of the slice: x: 4, y: 4, z: 8, core: 2. Of those that a mesh axis runs over, the one named last changes fastest.
Arguments:
- left_factor: bfloat16 [64, 32, 2048, 128], P('prow', 'pcol'), may hold values from -0.8984375 to 0.8984375
- right_factor: bfloat16 [64, 32, 2048, 128], P('prow', 'pcol'), may hold values from -0.8984375 to 0.8984375
- pivot_left: bfloat16 [32, 2048, 128], P('pcol', 'prow'), may hold values from -0.8984375 to 0.8984375
- pivot_right: bfloat16 [32, 2048, 128], P('pcol', 'prow'), may hold values from -0.8984375 to 0.8984375
- target_left: bfloat16 [2048, 64, 128], P('pcol', 'prow'), may hold values from -6 to 6
- target_right: bfloat16 [2048, 64, 128], P('pcol', 'prow'), may hold values from -6 to 6
- probe: bfloat16 [2048, 128], P('prow'), may hold values from -6 to 6
- ranks: int32 [64, 32], P('prow', 'pcol'), may hold values from 16 to 128
Outputs:
- basis: float32 [2048, 64, 128], P('pcol', 'prow')
- coefficient: float32 [2048, 64, 128], P('pcol', 'prow')
The draws below stay inside these ranges and needn't reach their ends.
All inputs are finite; a program needn't handle non-finite values.
Results may differ from the reference program's by a relative error of at most 0.0038.
Values may be sent and summed in bfloat16 or wider, within the bound.
No kernel may reach another device: no remote copies, remote signals or barrier semaphores. Data moves between devices by JAX's collectives and lax.ppermute only.
A program may use at most 64 MiB of HBM per device.

```python
from functools import partial
import jax
import jax.numpy as jnp
from jax import lax

B = 2048
R = 128
NT = 64
NC = 32


def with_ends(values, stream_key, least, top_value):
    index_at = [jax.random.randint(jax.random.fold_in(stream_key, axis), (), 0, length) for axis, length in enumerate(values.shape)]
    widest = values.shape.index(max(values.shape))
    beside = index_at[:widest] + [(index_at[widest] + 1) % values.shape[widest]] + index_at[widest + 1:]
    return values.at[tuple(index_at)].set(least).at[tuple(beside)].set(top_value)


def block_scale(stream_key, extent, shards, least, largest):
    loudness = 1.0
    for position, parts in shards:
        heights = jax.random.uniform(jax.random.fold_in(jax.random.fold_in(stream_key, 6), position), (parts,), jnp.float32, least / len(shards), largest / len(shards))
        loudness = loudness * jnp.repeat(jnp.exp(heights), extent[position] // parts).reshape((-1,) + (1,) * (len(extent) - 1 - position))
    return loudness


def scatter_about(stream_key, extent, deviation, bound, pieces=(), dtype=jnp.bfloat16):
    array = deviation * jax.random.normal(stream_key, extent, jnp.float32)
    if pieces:
        array = array * block_scale(stream_key, extent, pieces, -0.22, 0.18)
    return jnp.clip(array, -bound, bound).astype(dtype)


def setup_inputs(seed: int = 0) -> dict:
    arg_keys = jax.random.split(jax.random.key(seed), 9)
    return {
        "left_factor": scatter_about(arg_keys[0], (NT, NC, B, R), 0.15, 0.8984375, ((0, 16), (1, 16))),
        "right_factor": scatter_about(arg_keys[1], (NT, NC, B, R), 0.15, 0.8984375, ((0, 16), (1, 16))),
        "pivot_left": scatter_about(arg_keys[2], (NC, B, R), 0.15, 0.8984375, ((0, 16), (1, 16))),
        "pivot_right": scatter_about(arg_keys[3], (NC, B, R), 0.15, 0.8984375, ((0, 16), (1, 16))),
        "target_left": scatter_about(arg_keys[4], (B, NT, R), 1.0, 6.0, ((0, 16), (1, 16))),
        "target_right": scatter_about(arg_keys[5], (B, NT, R), 1.0, 6.0, ((0, 16), (1, 16))),
        "probe": scatter_about(arg_keys[6], (B, R), 1.0, 6.0, ((0, 16),)),
        "ranks": with_ends(jax.random.randint(arg_keys[7], (NT, NC), R // 8, R + 1), jax.random.fold_in(arg_keys[7], 1), R // 8, R).astype(jnp.int32),
    }


exact_mode = lax.Precision.HIGHEST

def one_target(pivot_sample, pivot_left, pivot_right, target_items):
    left_tile, right_tile, tile_ranks, plain_left, plain_right, target_sample = target_items
    rank_mask = (jnp.arange(R)[None, :] < tile_ranks[:, None]).astype(jnp.float32)
    coupling = jnp.einsum('jbr,jbs->jrs', right_tile.astype(jnp.float32), pivot_right.astype(jnp.float32))
    coupling = coupling * rank_mask[:, :, None]
    weights = jnp.einsum('jrs,jst->jrt', coupling, pivot_sample, precision=exact_mode).astype(jnp.bfloat16)
    direct = jnp.einsum('bs,st->bt', plain_left.astype(jnp.float32), target_sample, precision=exact_mode)
    update = jnp.einsum('jbr,jrt->bt', left_tile.astype(jnp.float32), weights.astype(jnp.float32))
    samples = direct - update
    gram_matrix = jnp.dot(samples.T, samples, precision=exact_mode) / B
    lower_factor = jnp.linalg.cholesky(gram_matrix)
    basis_tile = lax.linalg.triangular_solve(lower_factor, samples, left_side=False, lower=True, transpose_a=True)
    basis_half = basis_tile.astype(jnp.bfloat16)
    correlation = jnp.einsum('jbr,bt->jrt', left_tile.astype(jnp.float32), basis_half.astype(jnp.float32))
    reduced = jnp.einsum('jrs,jrt->jst', coupling, correlation, precision=exact_mode).astype(jnp.bfloat16)
    target_correlation = jnp.einsum('bs,bt->st', plain_left.astype(jnp.float32), basis_half.astype(jnp.float32)).astype(jnp.bfloat16)
    own_term = jnp.einsum('bs,st->bt', plain_right.astype(jnp.float32), target_correlation.astype(jnp.float32))
    pivot_term = jnp.einsum('jbs,jst->bt', pivot_left.astype(jnp.float32), reduced.astype(jnp.float32))
    coefficient = (own_term - pivot_term) / B
    return (basis_tile, coefficient)

def reference(left_factor, right_factor, pivot_left, pivot_right, target_left, target_right, probe, ranks):
    probe_wide = probe.astype(jnp.float32)
    pivot_sample = jnp.einsum('jbr,bs->jrs', pivot_left.astype(jnp.float32), probe_wide)
    target_sample = jnp.einsum('bir,bs->irs', target_right.astype(jnp.float32), probe_wide)
    target_items = (left_factor, right_factor, ranks, jnp.transpose(target_left, (1, 0, 2)), jnp.transpose(target_right, (1, 0, 2)), target_sample)
    basis_all, coefficient_all = lax.map(partial(one_target, pivot_sample, pivot_left, pivot_right), target_items)
    return (jnp.transpose(basis_all, (1, 0, 2)), jnp.transpose(coefficient_all, (1, 0, 2)))
```

```python
import jax
import jax.numpy as jnp
from jax import lax
from jax.experimental import pallas as pl
from jax.experimental.pallas import tpu as pltpu
from jax.sharding import PartitionSpec as P


HI = lax.Precision.HIGHEST
F32 = jnp.float32
BF = jnp.bfloat16
SIDE = 4
CHIPS = 8
CORES = 2
NB = 32


def dims(a, b, ca, cb, precision=None):
    return lax.dot_general(
        a, b, (((ca,), (cb,)), ((), ())), precision=precision, preferred_element_type=F32
    )


def to_sibling(v):
    return lax.ppermute(v, "pcol", [(i, i ^ 1) for i in range(CHIPS * CORES)])


def along_z(v, k):
    n = CHIPS * CORES
    return lax.ppermute(v, "pcol", [(i, (i + CORES * k) % n) for i in range(n)])


def along_y(v, d):
    return lax.ppermute(
        v, "prow", [(SIDE * x + y, SIDE * x + (y + d) % SIDE) for x in range(SIDE) for y in range(SIDE)]
    )


def along_x(v, d):
    return lax.ppermute(
        v, "prow", [(SIDE * x + y, SIDE * ((x + d) % SIDE) + y) for x in range(SIDE) for y in range(SIDE)]
    )


def gather_plane(v):
    stacked = jnp.stack([v] + [along_y(v, d) for d in range(1, SIDE)])
    return [stacked] + [along_x(stacked, d) for d in range(1, SIDE)]


def sum_plane(v):
    v = v + along_y(v, 1) + along_y(v, 2) + along_y(v, 3)
    return v + along_x(v, 1) + along_x(v, 2) + along_x(v, 3)


def gather_line(v):
    own = [v] + [along_z(v, k) for k in range(1, CHIPS)]
    return own + [to_sibling(b) for b in own]


def scatter_line(keep, send):
    return combine(keep, to_sibling(send))


def pair_kernel(keep, recv, own, *outs):
    own[...] = keep[0] + recv[0].astype(F32)
    for k, out in enumerate(outs, 1):
        out[...] = (keep[k] + recv[k].astype(F32)).astype(BF)


def combine(keep, recv):
    shape = keep.shape[1:]
    got = pl.pallas_call(
        pair_kernel,
        out_shape=[jax.ShapeDtypeStruct(shape, F32)]
        + [jax.ShapeDtypeStruct(shape, BF)] * (CHIPS - 1),
        name="pair_sum",
    )(keep, recv)
    return got[0], [along_z(v, k) for k, v in enumerate(got[1:], 1)]


def total(own, others):
    acc = own[...]
    for other in others:
        acc = acc + other[...].astype(F32)
    return acc


def samples_kernel(own, *refs):
    others, (wide, half) = refs[:-2], refs[-2:]
    acc = total(own, others)
    wide[...] = acc
    half[...] = acc.astype(BF)


def finish_kernel(own, *refs):
    others, out = refs[:-1], refs[-1]
    order = out.shape[0] * CHIPS * CORES
    for i in range(own.shape[0]):
        acc = own[i]
        for other in others:
            acc = acc + other[i].astype(F32)
        out[:, i, :] = acc * (1.0 / order)


def line_rows(q, k, sibling):
    core = q & 1
    chip = ((q >> 1) - k) & (CHIPS - 1)
    return chip * CORES + (core ^ sibling)


def forward_rows(q, k, sibling):
    core = q & 1
    chip = ((q >> 1) + k) & (CHIPS - 1)
    return chip * CORES + (core ^ sibling)


def place_line(q, pieces, whole):
    span = pieces[0].shape[1]
    for n, piece in enumerate(pieces):
        row = pl.multiple_of(line_rows(q, n % CHIPS, n // CHIPS) * span, span)
        whole[:, pl.ds(row, span), :] = piece[...]


def place_plane(p, pieces, whole):
    span = pieces[0].shape[2]
    for dx, piece in enumerate(pieces):
        for dy in range(SIDE):
            x = ((p >> 2) - dx) & (SIDE - 1)
            y = ((p & 3) - dy) & (SIDE - 1)
            row = pl.multiple_of((x * SIDE + y) * span, span)
            whole[:, pl.ds(row, span), :] = piece[dy]


def spread(q, i, source, keep, send):
    span = keep.shape[2]
    for k in range(CHIPS):
        row = pl.multiple_of(forward_rows(q, k, 0) * span, span)
        keep[k, i] = source[pl.ds(row, span), :]
        row = pl.multiple_of(forward_rows(q, k, 1) * span, span)
        send[k, i] = source[pl.ds(row, span), :].astype(BF)


def sample_kernel(tiles, columns):
    def kernel(p_ref, q_ref, ranks, left, right, ps, tright, probe, *refs):
        right_pieces, refs = refs[:SIDE], refs[SIDE:]
        line_pieces, refs = refs[: CHIPS * CORES], refs[CHIPS * CORES :]
        coupling, keep, send, whole, pivot, result = refs
        p, q = p_ref[0], q_ref[0]
        place_plane(p, right_pieces, pivot)
        place_line(q, line_pieces, whole)
        pivot_t = [pivot[j].T for j in range(columns)]
        for i in range(tiles):
            weights = []
            for j in range(columns):
                coup_t = dims(pivot_t[j], right[i, j], 1, 0)
                coup = coup_t.T
                row = lax.broadcasted_iota(jnp.int32, coup.shape, 0)
                coup = jnp.where(row < ranks[i, j], coup, 0.0)
                coupling[i, j] = coup
                weights.append((-dims(coup, ps[j], 1, 0, HI)).astype(BF))
            share = dims(tright[i], probe[...], 0, 0)
            high = share.astype(BF)
            low = (share - high.astype(F32)).astype(BF)
            u = jnp.concatenate([left[i, j] for j in range(columns)], axis=1)
            t = jnp.concatenate([whole[i], whole[i]], axis=1)
            result[...] = dims(u, jnp.concatenate(weights, axis=0), 1, 0) + dims(
                t, jnp.concatenate([high, low], axis=0), 1, 0
            )
            spread(q, i, result, keep, send)

    return kernel


def factor_inverse(gram):
    tiles, rank, _ = gram.shape
    a = gram
    row = lax.broadcasted_iota(jnp.int32, (NB, NB), 0)
    col = lax.broadcasted_iota(jnp.int32, (NB, NB), 1)
    inverse_rows = []
    for start in range(0, rank, NB):
        stop = start + NB
        m = [a[i][:NB, start:stop] for i in range(tiles)]
        for k in range(NB):
            below = row > k
            for i in range(tiles):
                pivot_row = m[i][k : k + 1, :]
                scaled = pivot_row * (1.0 / m[i][k : k + 1, k : k + 1])
                factor = jnp.where(below, m[i][:, k : k + 1], 0.0)
                inv = 1.0 / m[i][k : k + 1, k : k + 1]
                scaled = jnp.where(col[:1] == k, inv, scaled)
                base = jnp.where(below & (col == k), 0.0, m[i])
                m[i] = base - factor * scaled
        new_a = []
        rows_out = []
        for i in range(tiles):
            diagonal = jnp.sum(jnp.where(row == col, m[i], 0.0), axis=1, keepdims=True)
            unit = jnp.where(row == col, 1.0, jnp.where(row > col, m[i], 0.0))
            t = unit / jnp.sqrt(diagonal)
            line = dims(t, a[i][:NB, :], 1, 0, HI)
            wide = [line[:, :start], t, line[:, stop:]]
            line = jnp.concatenate([w for w in wide if w.shape[1]], axis=1)
            rows_out.append(line)
            if stop < rank:
                rest = a[i][NB:, :]
                lane = lax.broadcasted_iota(jnp.int32, rest.shape, 1)
                rest = jnp.where((lane >= start) & (lane < stop), 0.0, rest)
                new_a.append(rest - dims(line[:, stop:], line, 0, 0, HI))
        a = new_a
        inverse_rows.append(rows_out)
    out = []
    lane = lax.broadcasted_iota(jnp.int32, (rank, rank), 1)
    sub = lax.broadcasted_iota(jnp.int32, (rank, rank), 0)
    for i in range(tiles):
        full = jnp.concatenate([rows[i] for rows in inverse_rows], axis=0)
        out.append(jnp.where(lane <= sub, full, 0.0))
    return out


def project_kernel(tiles, columns):
    def kernel(p_ref, q_ref, left, coupling, target, tright, wide, *refs):
        line_pieces, refs = refs[: CHIPS * CORES], refs[CHIPS * CORES :]
        left_pieces, refs = refs[:SIDE], refs[SIDE:]
        basis, keep, send, pivot, whole, result = refs
        p, q = p_ref[0], q_ref[0]
        order = whole.shape[1]
        place_line(q, line_pieces, whole)
        place_plane(p, left_pieces, pivot)
        flipped = [whole[i].T for i in range(tiles)]
        gram = jnp.stack([dims(flipped[i], whole[i], 1, 0) * (1.0 / order) for i in range(tiles)])
        inverse = factor_inverse(gram)
        u = jnp.concatenate([pivot[j] for j in range(columns)], axis=1)
        for i in range(tiles):
            mixed = [
                dims(dims(flipped[i], left[i, j], 1, 0), coupling[i, j], 1, 0, HI)
                for j in range(columns)
            ]
            mixed.append(dims(flipped[i], target[i], 1, 0))
            solved = dims(inverse[i], jnp.concatenate(mixed, axis=1), 1, 0, HI).astype(BF)
            span = mixed[0].shape[1]
            reduced = solved[:, : columns * span]
            correlation = solved[:, columns * span :]
            basis[:, i, :] = dims(wide[i], inverse[i], 1, 1, HI)
            result[...] = -dims(u, reduced, 1, 1)
            spread(q, i, result, keep, send)
            keep[0, i] = keep[0, i] + dims(tright[i], correlation, 1, 1)

    return kernel


def vmem(n):
    return [pl.BlockSpec(memory_space=pltpu.VMEM)] * n


def smem(n):
    return [pl.BlockSpec(memory_space=pltpu.SMEM)] * n


def per_device(
    left_factor, right_factor, pivot_left, pivot_right, target_left, target_right, probe, ranks
):
    tiles, columns, order, rank = left_factor.shape
    span = target_left.shape[0]
    p = jnp.full((1,), lax.axis_index("prow"), jnp.int32)
    q = jnp.full((1,), lax.axis_index("pcol"), jnp.int32)
    n_row, n_col = SIDE * SIDE, CHIPS * CORES
    turned = [(a * n_col + b, b * n_col + a) for a in range(n_row) for b in range(n_col)]
    probe_own = lax.ppermute(probe, ("prow", "pcol"), turned)
    right_plane = gather_plane(pivot_right)
    part = jnp.einsum("jbr,bs->jrs", pivot_left, probe, preferred_element_type=F32)
    pivot_sample = sum_plane(part)
    left_line = gather_line(jnp.transpose(target_left, (1, 0, 2)))
    right_own = jnp.transpose(target_right, (1, 0, 2))

    share = (CHIPS, tiles, span, rank)
    coupling, keep, send, target = pl.pallas_call(
        sample_kernel(tiles, columns),
        out_shape=[
            jax.ShapeDtypeStruct((tiles, columns, rank, rank), F32),
            jax.ShapeDtypeStruct(share, F32),
            jax.ShapeDtypeStruct(share, BF),
            jax.ShapeDtypeStruct((tiles, order, rank), BF),
        ],
        in_specs=smem(3) + vmem(5 + SIDE + CHIPS * CORES),
        scratch_shapes=[pltpu.VMEM((columns, order, rank), BF), pltpu.VMEM((order, rank), F32)],
        name="sample",
    )(p, q, ranks, left_factor, right_factor, pivot_sample, right_own, probe_own, *right_plane, *left_line)

    pivot_late, send = lax.optimization_barrier((pivot_left, send))
    own, others = scatter_line(keep, send)
    left_plane = gather_plane(pivot_late)
    wide, half = pl.pallas_call(
        samples_kernel,
        out_shape=[jax.ShapeDtypeStruct(own.shape, F32), jax.ShapeDtypeStruct(own.shape, BF)],
        name="samples_sum",
    )(own, *others)
    sample_line = gather_line(half)

    basis, keep, send = pl.pallas_call(
        project_kernel(tiles, columns),
        out_shape=[
            jax.ShapeDtypeStruct((span, tiles, rank), F32),
            jax.ShapeDtypeStruct(share, F32),
            jax.ShapeDtypeStruct(share, BF),
        ],
        in_specs=smem(2) + vmem(5 + SIDE + CHIPS * CORES),
        scratch_shapes=[
            pltpu.VMEM((columns, order, rank), BF),
            pltpu.VMEM((tiles, order, rank), BF),
            pltpu.VMEM((order, rank), F32),
        ],
        name="project",
    )(p, q, left_factor, coupling, target, right_own, wide, *sample_line, *left_plane)
    own, others = scatter_line(keep, send)
    coefficient = pl.pallas_call(
        finish_kernel,
        out_shape=jax.ShapeDtypeStruct((span, tiles, rank), F32),
        name="finish",
    )(own, *others)
    return (basis, coefficient)


def solution(mesh):
    in_specs = (
        P("prow", "pcol", None, None),
        P("prow", "pcol", None, None),
        P("pcol", "prow", None),
        P("pcol", "prow", None),
        P("pcol", "prow", None),
        P("pcol", "prow", None),
        P("prow", None),
        P("prow", "pcol"),
    )
    out_specs = (P("pcol", "prow", None), P("pcol", "prow", None))
    return jax.shard_map(
        per_device, mesh=mesh, in_specs=in_specs, out_specs=out_specs, check_vma=False
    )
```

```python
import jax
import jax.numpy as jnp
from jax import lax
from jax.experimental import pallas as pl
from jax.experimental.pallas import tpu as pltpu
from jax.sharding import PartitionSpec as P


HI = lax.Precision.HIGHEST
F32 = jnp.float32
BF = jnp.bfloat16
SIDE = 4
CHIPS = 8
CORES = 2
NB = 32


def dims(a, b, ca, cb, precision=None):
    return lax.dot_general(
        a, b, (((ca,), (cb,)), ((), ())), precision=precision, preferred_element_type=F32
    )


def to_sibling(v):
    return lax.ppermute(v, "pcol", [(i, i ^ 1) for i in range(CHIPS * CORES)])


def along_z(v, k):
    n = CHIPS * CORES
    return lax.ppermute(v, "pcol", [(i, (i + CORES * k) % n) for i in range(n)])


def along_y(v, d):
    return lax.ppermute(
        v, "prow", [(SIDE * x + y, SIDE * x + (y + d) % SIDE) for x in range(SIDE) for y in range(SIDE)]
    )


def along_x(v, d):
    return lax.ppermute(
        v, "prow", [(SIDE * x + y, SIDE * ((x + d) % SIDE) + y) for x in range(SIDE) for y in range(SIDE)]
    )


def gather_plane(v):
    stacked = jnp.stack([v] + [along_y(v, d) for d in range(1, SIDE)])
    return [stacked] + [along_x(stacked, d) for d in range(1, SIDE)]


def sum_plane(v):
    v = v + along_y(v, 1) + along_y(v, 2) + along_y(v, 3)
    return v + along_x(v, 1) + along_x(v, 2) + along_x(v, 3)


def gather_line(v):
    right, left, up, down = [v], [], v, v
    for step in range(CHIPS // 2):
        up = along_z(up, 1)
        right.append(up)
        if step < CHIPS // 2 - 1:
            down = along_z(down, -1)
            left.insert(0, down)
    own = right + left
    return own + [to_sibling(b) for b in own]


def scatter_line(keep, send):
    other = to_sibling(send)

    def share(k):
        return keep[k] + other[k].astype(F32)

    half = CHIPS // 2
    up, down = share(half).astype(BF), share(half + 1).astype(BF)
    for k in range(half - 1, 0, -1):
        up = (along_z(up, 1).astype(F32) + share(k)).astype(BF)
        down = along_z(down, -1)
        if k > 1:
            down = (down.astype(F32) + share(CHIPS - k + 1)).astype(BF)
    return share(0), along_z(up, 1), down


def samples_kernel(own, up, down, wide, half):
    acc = own[...] + up[...].astype(F32) + down[...].astype(F32)
    wide[...] = acc
    half[...] = acc.astype(BF)


def finish_kernel(own, up, down, out):
    order = out.shape[0] * CHIPS * CORES
    for i in range(own.shape[0]):
        acc = own[i] + up[i].astype(F32) + down[i].astype(F32)
        out[:, i, :] = acc * (1.0 / order)


def deal_kernel(left_t, right_t, probe, out):
    tiles, rank, _ = left_t.shape
    span = rank // out.shape[0]
    for i in range(tiles):
        left, right = left_t[i].astype(F32), right_t[i].astype(F32)
        part = dims(right_t[i], probe[...], 1, 0)
        high = part.astype(BF).astype(F32)
        low = part - high
        for n in range(out.shape[0]):
            rows = slice(n * span, (n + 1) * span)
            out[n, i] = jnp.concatenate([left[rows], right[rows]], axis=0).astype(BF)
            out[n, tiles + i] = jnp.concatenate([high[rows], low[rows]], axis=0).astype(BF)


def line_rows(q, k, sibling):
    core = q & 1
    chip = ((q >> 1) - k) & (CHIPS - 1)
    return chip * CORES + (core ^ sibling)


def forward_rows(q, k, sibling):
    core = q & 1
    chip = ((q >> 1) + k) & (CHIPS - 1)
    return chip * CORES + (core ^ sibling)


def place_line(q, pieces, whole):
    span = pieces[0].shape[1]
    for n, piece in enumerate(pieces):
        row = pl.multiple_of(line_rows(q, n % CHIPS, n // CHIPS) * span, span)
        whole[:, pl.ds(row, span), :] = piece[...]


def place_plane(p, pieces, whole):
    span = pieces[0].shape[2]
    for dx, piece in enumerate(pieces):
        for dy in range(SIDE):
            x = ((p >> 2) - dx) & (SIDE - 1)
            y = ((p & 3) - dy) & (SIDE - 1)
            row = pl.multiple_of((x * SIDE + y) * span, span)
            whole[:, pl.ds(row, span), :] = piece[dy]


def spread(q, i, source, keep, send):
    span = keep.shape[2]
    for k in range(CHIPS):
        row = pl.multiple_of(forward_rows(q, k, 0) * span, span)
        keep[k, i] = source[pl.ds(row, span), :]
        row = pl.multiple_of(forward_rows(q, k, 1) * span, span)
        send[k, i] = source[pl.ds(row, span), :].astype(BF)


def own_ranks(dealt, i):
    return jnp.concatenate([dealt[n, i] for n in range(dealt.shape[0])], axis=1)


def sample_kernel(tiles, columns):
    def kernel(p_ref, q_ref, ranks, left, right, ps, dealt, *refs):
        right_pieces, refs = refs[:SIDE], refs[SIDE:]
        coupling, keep, send, pivot, pivot_t, result = refs
        p, q = p_ref[0], q_ref[0]
        place_plane(p, right_pieces, pivot)
        for j in range(columns):
            pivot_t[j] = pivot[j].T

        def tile(i, carry):
            weights = []
            for j in range(columns):
                coup = dims(pivot_t[j], right[i, j], 1, 0).T
                row = lax.broadcasted_iota(jnp.int32, coup.shape, 0)
                coup = jnp.where(row < ranks[i, j], coup, 0.0)
                coupling[i, j] = coup
                weights.append((-dims(coup, ps[j], 1, 0, HI)).astype(BF))
            both = jnp.sum(dealt[:, tiles + i].astype(F32), axis=0)
            span = both.shape[0] // 2
            share = both[:span] + both[span:]
            high = share.astype(BF).astype(F32)
            zero = jnp.zeros_like(share)
            share = jnp.concatenate([high, zero, share - high, zero], axis=0).astype(BF)
            own = own_ranks(dealt, i)
            u = jnp.concatenate([left[i, j] for j in range(columns)], axis=1)
            result[...] = dims(u, jnp.concatenate(weights, axis=0), 1, 0) + dims(
                jnp.concatenate([own, own], axis=0), share, 0, 0
            )
            spread(q, i, result, keep, send)
            return carry

        lax.fori_loop(0, tiles, tile, 0)

    return kernel


def factor_inverse(gram):
    tiles, rank, _ = gram.shape
    a = gram
    row = lax.broadcasted_iota(jnp.int32, (NB, NB), 0)
    col = lax.broadcasted_iota(jnp.int32, (NB, NB), 1)
    inverse_rows = []
    for start in range(0, rank, NB):
        stop = start + NB
        m = [a[i][:NB, start:stop] for i in range(tiles)]
        for k in range(NB):
            below = row > k
            for i in range(tiles):
                pivot_row = m[i][k : k + 1, :]
                scaled = pivot_row * (1.0 / m[i][k : k + 1, k : k + 1])
                factor = jnp.where(below, m[i][:, k : k + 1], 0.0)
                inv = 1.0 / m[i][k : k + 1, k : k + 1]
                scaled = jnp.where(col[:1] == k, inv, scaled)
                base = jnp.where(below & (col == k), 0.0, m[i])
                m[i] = base - factor * scaled
        new_a = []
        rows_out = []
        for i in range(tiles):
            diagonal = jnp.sum(jnp.where(row == col, m[i], 0.0), axis=1, keepdims=True)
            unit = jnp.where(row == col, 1.0, jnp.where(row > col, m[i], 0.0))
            t = unit / jnp.sqrt(diagonal)
            line = dims(t, a[i][:NB, :], 1, 0, HI)
            wide = [line[:, :start], t, line[:, stop:]]
            line = jnp.concatenate([w for w in wide if w.shape[1]], axis=1)
            rows_out.append(line)
            if stop < rank:
                rest = a[i][NB:, :]
                lane = lax.broadcasted_iota(jnp.int32, rest.shape, 1)
                rest = jnp.where((lane >= start) & (lane < stop), 0.0, rest)
                new_a.append(rest - dims(line[:, stop:], line, 0, 0, HI))
        a = new_a
        inverse_rows.append(rows_out)
    out = []
    lane = lax.broadcasted_iota(jnp.int32, (rank, rank), 1)
    sub = lax.broadcasted_iota(jnp.int32, (rank, rank), 0)
    for i in range(tiles):
        full = jnp.concatenate([rows[i] for rows in inverse_rows], axis=0)
        out.append(jnp.where(lane <= sub, full, 0.0))
    return out


def project_kernel(tiles, columns):
    def kernel(p_ref, q_ref, left, coupling, dealt, wide, *refs):
        line_pieces, refs = refs[: CHIPS * CORES], refs[CHIPS * CORES :]
        left_pieces, refs = refs[:SIDE], refs[SIDE:]
        basis, keep, send, pivot, whole, flipped, gram, result = refs
        p, q = p_ref[0], q_ref[0]
        order = whole.shape[1]
        place_line(q, line_pieces, whole)
        place_plane(p, left_pieces, pivot)

        def square(i, carry):
            flipped[i] = whole[i].T
            gram[i] = dims(flipped[i], whole[i], 1, 0) * (1.0 / order)
            return carry

        lax.fori_loop(0, tiles, square, 0)
        for i, inverse in enumerate(factor_inverse(gram[...])):
            gram[i] = inverse
            basis[:, i, :] = dims(wide[i], inverse, 1, 1, HI)

        def tile(i, carry):
            inverse = gram[i]
            mixed = [
                dims(dims(flipped[i], left[i, j], 1, 0), coupling[i, j], 1, 0, HI)
                for j in range(columns)
            ]
            reduced = dims(inverse, jnp.concatenate(mixed, axis=1), 1, 0, HI).astype(BF)
            own = own_ranks(dealt, i)
            seen = dims(dims(own, whole[i], 1, 0), inverse, 1, 1, HI)
            span = seen.shape[0] // 2
            seen = jnp.concatenate([jnp.zeros_like(seen[:span]), seen[:span]], axis=0).astype(BF)
            u = jnp.concatenate([pivot[j] for j in range(columns)], axis=1)
            result[...] = dims(own, seen, 0, 0) - dims(u, reduced, 1, 1)
            spread(q, i, result, keep, send)
            return carry

        lax.fori_loop(0, tiles, tile, 0)

    return kernel


def vmem(n):
    return [pl.BlockSpec(memory_space=pltpu.VMEM)] * n


def smem(n):
    return [pl.BlockSpec(memory_space=pltpu.SMEM)] * n


def per_device(
    left_factor, right_factor, pivot_left, pivot_right, target_left, target_right, probe, ranks
):
    tiles, columns, order, rank = left_factor.shape
    span = target_left.shape[0]
    p = jnp.full((1,), lax.axis_index("prow"), jnp.int32)
    q = jnp.full((1,), lax.axis_index("pcol"), jnp.int32)
    n_row, n_col = SIDE * SIDE, CHIPS * CORES
    turned = [(a * n_col + b, b * n_col + a) for a in range(n_row) for b in range(n_col)]
    probe_own = lax.ppermute(probe, ("prow", "pcol"), turned)
    right_plane = gather_plane(pivot_right)
    part = jnp.einsum("jbr,bs->jrs", pivot_left, probe, preferred_element_type=F32)
    pivot_sample = sum_plane(part)
    dealt = pl.pallas_call(
        deal_kernel,
        out_shape=jax.ShapeDtypeStruct((n_col, 2 * tiles, 2 * rank // n_col, span), BF),
        name="deal",
    )(jnp.transpose(target_left, (1, 2, 0)), jnp.transpose(target_right, (1, 2, 0)), probe_own)
    dealt = lax.all_to_all(dealt, "pcol", 0, 0, tiled=True)

    share = (CHIPS, tiles, span, rank)
    coupling, keep, send = pl.pallas_call(
        sample_kernel(tiles, columns),
        out_shape=[
            jax.ShapeDtypeStruct((tiles, columns, rank, rank), F32),
            jax.ShapeDtypeStruct(share, F32),
            jax.ShapeDtypeStruct(share, BF),
        ],
        in_specs=smem(3) + vmem(4 + SIDE),
        scratch_shapes=[
            pltpu.VMEM((columns, order, rank), BF),
            pltpu.VMEM((columns, rank, order), BF),
            pltpu.VMEM((order, rank), F32),
        ],
        name="sample",
    )(p, q, ranks, left_factor, right_factor, pivot_sample, dealt, *right_plane)

    pivot_late, send = lax.optimization_barrier((pivot_left, send))
    left_plane = gather_plane(pivot_late)
    parts = scatter_line(keep, send)
    wide, half = pl.pallas_call(
        samples_kernel,
        out_shape=[jax.ShapeDtypeStruct(share[1:], F32), jax.ShapeDtypeStruct(share[1:], BF)],
        name="samples_sum",
    )(*parts)
    sample_line = gather_line(half)

    basis, keep, send = pl.pallas_call(
        project_kernel(tiles, columns),
        out_shape=[
            jax.ShapeDtypeStruct((span, tiles, rank), F32),
            jax.ShapeDtypeStruct(share, F32),
            jax.ShapeDtypeStruct(share, BF),
        ],
        in_specs=smem(2) + vmem(4 + SIDE + CHIPS * CORES),
        scratch_shapes=[
            pltpu.VMEM((columns, order, rank), BF),
            pltpu.VMEM((tiles, order, rank), BF),
            pltpu.VMEM((tiles, rank, order), BF),
            pltpu.VMEM((tiles, rank, rank), F32),
            pltpu.VMEM((order, rank), F32),
        ],
        name="project",
    )(p, q, left_factor, coupling, dealt, wide, *sample_line, *left_plane)
    coefficient = pl.pallas_call(
        finish_kernel,
        out_shape=jax.ShapeDtypeStruct((span, tiles, rank), F32),
        name="finish",
    )(*scatter_line(keep, send))
    return (basis, coefficient)


def solution(mesh):
    in_specs = (
        P("prow", "pcol", None, None),
        P("prow", "pcol", None, None),
        P("pcol", "prow", None),
        P("pcol", "prow", None),
        P("pcol", "prow", None),
        P("pcol", "prow", None),
        P("prow", None),
        P("prow", "pcol"),
    )
    out_specs = (P("pcol", "prow", None), P("pcol", "prow", None))
    return jax.shard_map(
        per_device, mesh=mesh, in_specs=in_specs, out_specs=out_specs, check_vma=False
    )
```

```python
import jax
import jax.numpy as jnp
from jax import lax
from jax.experimental import pallas as pl
from jax.experimental.pallas import tpu as pltpu
from jax.sharding import PartitionSpec as P


HI = lax.Precision.HIGHEST
F32 = jnp.float32
BF = jnp.bfloat16
SIDE = 4
CHIPS = 8
CORES = 2
NB = 32


def dims(a, b, ca, cb, precision=None):
    return lax.dot_general(
        a, b, (((ca,), (cb,)), ((), ())), precision=precision, preferred_element_type=F32
    )


def halves(v):
    high = v.astype(BF)
    return high, (v - high.astype(F32)).astype(BF)


def fine(a, b, ca, cb):
    ah, al = halves(a)
    bh, bl = halves(b)
    return dims(ah, bh, ca, cb) + (dims(ah, bl, ca, cb) + dims(al, bh, ca, cb))


def to_sibling(v):
    return lax.ppermute(v, "pcol", [(i, i ^ 1) for i in range(CHIPS * CORES)])


def along_z(v, k):
    n = CHIPS * CORES
    return lax.ppermute(v, "pcol", [(i, (i + CORES * k) % n) for i in range(n)])


def along_y(v, d):
    return lax.ppermute(
        v, "prow", [(SIDE * x + y, SIDE * x + (y + d) % SIDE) for x in range(SIDE) for y in range(SIDE)]
    )


def along_x(v, d):
    return lax.ppermute(
        v, "prow", [(SIDE * x + y, SIDE * ((x + d) % SIDE) + y) for x in range(SIDE) for y in range(SIDE)]
    )


def gather_plane(v):
    near, far = along_y(v, 1), along_y(v, -1)
    stacked = jnp.stack([v, near, along_y(v, 2), far])
    left = along_x(stacked, 1)
    right = along_x(stacked, -1)
    return [stacked, left, along_x(stacked[:, :1], 2), along_x(right[:, 1:], -1), right]


def sum_plane(v):
    v = v + along_x(v, 1) + along_x(v, -1) + along_x(v, 2)
    return v + along_y(v, 1) + along_y(v, -1) + along_y(v, 2)


def gather_line(v):
    right, left, up, down = [v], [], v, v
    for step in range(CHIPS // 2):
        up = along_z(up, 1)
        right.append(up)
        if step < CHIPS // 2 - 1:
            down = along_z(down, -1)
            left.insert(0, down)
    own = right + left
    return own + [to_sibling(b) for b in own]


def scatter_line(keep, send, down_type):
    other = to_sibling(send)

    def share(k):
        return keep[k] + other[k].astype(F32)

    half = CHIPS // 2
    up, down = share(half).astype(BF), share(half + 1).astype(down_type)
    for k in range(half - 1, 0, -1):
        up = (along_z(up, 1).astype(F32) + share(k)).astype(BF)
        down = along_z(down, -1)
        if k > 1:
            down = (down.astype(F32) + share(CHIPS - k + 1)).astype(down_type)
    return share(0), along_z(up, 1), down


def samples_kernel(own, up, down, wide, half):
    acc = own[...] + up[...].astype(F32) + down[...].astype(F32)
    wide[...] = acc
    half[...] = acc.astype(BF)


def finish_kernel(own, up, down, out):
    order = out.shape[0] * CHIPS * CORES
    for i in range(own.shape[0]):
        acc = own[i] + up[i].astype(F32) + down[i].astype(F32)
        out[:, i, :] = acc * (1.0 / order)


def line_rows(q, k, sibling):
    core = q & 1
    chip = ((q >> 1) - k) & (CHIPS - 1)
    return chip * CORES + (core ^ sibling)


def forward_rows(q, k, sibling):
    core = q & 1
    chip = ((q >> 1) + k) & (CHIPS - 1)
    return chip * CORES + (core ^ sibling)


def place_line(q, pieces, whole):
    span = pieces[0].shape[1]
    for n, piece in enumerate(pieces):
        row = pl.multiple_of(line_rows(q, n % CHIPS, n // CHIPS) * span, span)
        whole[:, pl.ds(row, span), :] = piece[...]


def place_plane(p, pieces, whole):
    span = pieces[0].shape[2]
    first, left, even, odd, right = pieces
    parts = [(first, 0, 0, 2), (left, 1, 0, 2), (even, 2, 0, 1), (odd, 2, 1, 2), (right, 3, 0, 2)]
    for piece, dx, start, stop in parts:
        for dy in range(SIDE):
            x = ((p >> 2) - dx) & (SIDE - 1)
            y = ((p & 3) - dy) & (SIDE - 1)
            row = pl.multiple_of((x * SIDE + y) * span, span)
            whole[start:stop, pl.ds(row, span), :] = piece[dy]


def spread(q, i, source, keep, send):
    span = keep.shape[2]
    for k in range(CHIPS):
        row = pl.multiple_of(forward_rows(q, k, 0) * span, span)
        keep[k, i] = source[pl.ds(row, span), :]
        row = pl.multiple_of(forward_rows(q, k, 1) * span, span)
        send[k, i] = source[pl.ds(row, span), :].astype(BF)


PIECES = SIDE + 1


def sample_kernel(tiles, columns):
    def kernel(p_ref, q_ref, ranks, left, right, ps, tright, probe, *refs):
        right_pieces, refs = refs[:PIECES], refs[PIECES:]
        line_pieces, refs = refs[: CHIPS * CORES], refs[CHIPS * CORES :]
        coupling, keep, send, whole, pivot, pivot_t, result = refs
        p, q = p_ref[0], q_ref[0]
        place_plane(p, right_pieces, pivot)
        place_line(q, line_pieces, whole)
        for j in range(columns):
            pivot_t[j] = pivot[j].T

        def tile(i, carry):
            weights = []
            for j in range(columns):
                coup = dims(pivot_t[j], right[i, j], 1, 0).T
                row = lax.broadcasted_iota(jnp.int32, coup.shape, 0)
                coup = jnp.where(row < ranks[i, j], coup, 0.0)
                coupling[i, j] = coup
                weights.append((-fine(coup, ps[j], 1, 0)).astype(BF))
            u = jnp.concatenate([left[i, j] for j in range(columns)], axis=1)
            t = jnp.concatenate([whole[i], whole[i]], axis=1)
            share = jnp.concatenate(halves(dims(tright[i], probe[...], 0, 0)), axis=0)
            result[...] = dims(u, jnp.concatenate(weights, axis=0), 1, 0) + dims(t, share, 1, 0)
            spread(q, i, result, keep, send)
            return carry

        lax.fori_loop(0, tiles, tile, 0)

    return kernel


def eliminate(m, width):
    lane = lax.broadcasted_iota(jnp.int32, (8, width), 1)
    sub = lax.broadcasted_iota(jnp.int32, (8, width), 0)
    within = lane & (NB - 1)
    base = lane - within
    for k in range(0, NB, 2):
        b, r = k // 8, k % 8
        at0, at1 = within == k, within == k + 1
        g0 = [jnp.take_along_axis(m[n], base + k, axis=1) if n >= b else None for n in range(len(m))]
        g1 = [jnp.take_along_axis(m[n], base + (k + 1), axis=1) if n >= b else None for n in range(len(m))]
        row0, row1 = m[b][r : r + 1], m[b][r + 1 : r + 2]
        i0 = 1.0 / g0[b][r : r + 1]
        up, low = g1[b][r : r + 1], g0[b][r + 1 : r + 2]
        ratio = up * i0
        i1 = 1.0 / (g1[b][r + 1 : r + 2] - low * ratio)
        at0r, at1r = at0[:1], at1[:1]
        s0 = jnp.where(at0r, i0, row0 * i0)
        next_row = jnp.where(at0r, 0.0, row1) - low * s0
        s1 = jnp.where(at1r, i1, next_row * i1)
        s0 = jnp.where(at1r, 0.0, s0)
        for n in range(b, len(m)):
            new = jnp.where(at0 | at1, 0.0, m[n]) - g0[n] * s0 - (g1[n] - g0[n] * ratio) * s1
            if n == b:
                new = jnp.where(sub > r + 1, new, jnp.where(sub == r + 1, next_row, m[n]))
            m[n] = new
    return m


def factor_inverse(gram):
    tiles, rank, _ = gram.shape
    width = tiles * NB
    lane = lax.broadcasted_iota(jnp.int32, (NB, width), 1)
    row = lax.broadcasted_iota(jnp.int32, (NB, width), 0)
    within = lane & (NB - 1)
    square_row = lax.broadcasted_iota(jnp.int32, (width, width), 0)
    square_lane = lax.broadcasted_iota(jnp.int32, (width, width), 1)
    same = (square_row & -NB) == (square_lane & -NB)
    full_lane = lax.broadcasted_iota(jnp.int32, (rank, rank), 1)
    for start in range(0, rank, NB):
        stop = start + NB
        block = slice(start, stop)
        packed = jnp.concatenate([gram[i, block, block] for i in range(tiles)], axis=1)
        m = eliminate([packed[n : n + 8] for n in range(0, NB, 8)], width)
        m = jnp.concatenate(m, axis=0)
        pivots = jnp.take_along_axis(m, lane - within + row, axis=1)
        unit = jnp.where(within == row, 1.0, jnp.where(within < row, m, 0.0)) / jnp.sqrt(pivots)
        diagonal = jnp.where(same, jnp.concatenate([unit] * tiles, axis=0), 0.0)
        lines = dims(diagonal, jnp.concatenate([gram[i, block, :] for i in range(tiles)], axis=0), 1, 0, HI)
        for i in range(tiles):
            line = lines[i * NB : (i + 1) * NB]
            own = pltpu.roll(unit, (start - i * NB) % width, 1) if (start - i * NB) % width else unit
            inside = (lane >= start) & (lane < stop)
            line = jnp.where(inside, own, line)
            gram[i, block, :] = jnp.where(lane < stop, line, 0.0)
            if stop < rank:
                update = dims(line, line, 0, 0, HI)[stop:]
                rest = gram[i, stop:, :]
                zero = (full_lane[stop:] >= start) & (full_lane[stop:] < stop)
                gram[i, stop:, :] = jnp.where(zero, 0.0, rest) - update


def project_kernel(tiles, columns):
    def kernel(p_ref, q_ref, left, coupling, target, tright, wide, *refs):
        line_pieces, refs = refs[: CHIPS * CORES], refs[CHIPS * CORES :]
        left_pieces, refs = refs[:PIECES], refs[PIECES:]
        basis, keep, send, pivot, whole, flipped, gram, result = refs
        p, q = p_ref[0], q_ref[0]
        order = whole.shape[1]
        place_line(q, line_pieces, whole)
        place_plane(p, left_pieces, pivot)

        def square(i, carry):
            flipped[i] = whole[i].T
            gram[i] = dims(flipped[i], whole[i], 1, 0) * (1.0 / order)
            return carry

        lax.fori_loop(0, tiles, square, 0)
        factor_inverse(gram)
        for i in range(tiles):
            basis[:, i, :] = fine(wide[i], gram[i], 1, 1)

        def tile(i, carry):
            inverse = gram[i]
            both = jnp.concatenate([left[i, j] for j in range(columns)], axis=1)
            seen = dims(flipped[i], both, 1, 0)
            span = inverse.shape[1]
            mixed = [
                fine(seen[:, j * span : (j + 1) * span], coupling[i, j], 1, 0) for j in range(columns)
            ]
            mixed.append(dims(flipped[i], target[i], 1, 0))
            solved = fine(inverse, jnp.concatenate(mixed, axis=1), 1, 0).astype(BF)
            u = jnp.concatenate([pivot[j] for j in range(columns)], axis=1)
            result[...] = -dims(u, solved[:, : columns * span], 1, 1)
            spread(q, i, result, keep, send)
            keep[0, i] = keep[0, i] + dims(tright[i], solved[:, columns * span :], 1, 1)
            return carry

        lax.fori_loop(0, tiles, tile, 0)

    return kernel


def vmem(n):
    return [pl.BlockSpec(memory_space=pltpu.VMEM)] * n


def smem(n):
    return [pl.BlockSpec(memory_space=pltpu.SMEM)] * n


def per_device(
    left_factor, right_factor, pivot_left, pivot_right, target_left, target_right, probe, ranks
):
    tiles, columns, order, rank = left_factor.shape
    span = target_left.shape[0]
    p = jnp.full((1,), lax.axis_index("prow"), jnp.int32)
    q = jnp.full((1,), lax.axis_index("pcol"), jnp.int32)
    n_row, n_col = SIDE * SIDE, CHIPS * CORES
    turned = [(a * n_col + b, b * n_col + a) for a in range(n_row) for b in range(n_col)]
    probe_own = lax.ppermute(probe, ("prow", "pcol"), turned)
    right_plane = gather_plane(pivot_right)
    part = jnp.einsum("jbr,bs->jrs", pivot_left, probe, preferred_element_type=F32)
    pivot_sample = sum_plane(part)
    left_line = gather_line(jnp.transpose(target_left, (1, 0, 2)))
    right_own = jnp.transpose(target_right, (1, 0, 2))

    share = (CHIPS, tiles, span, rank)
    coupling, keep, send, target = pl.pallas_call(
        sample_kernel(tiles, columns),
        out_shape=[
            jax.ShapeDtypeStruct((tiles, columns, rank, rank), F32),
            jax.ShapeDtypeStruct(share, F32),
            jax.ShapeDtypeStruct(share, BF),
            jax.ShapeDtypeStruct((tiles, order, rank), BF),
        ],
        in_specs=smem(3) + vmem(5 + PIECES + CHIPS * CORES),
        scratch_shapes=[
            pltpu.VMEM((columns, order, rank), BF),
            pltpu.VMEM((columns, rank, order), BF),
            pltpu.VMEM((order, rank), F32),
        ],
        name="sample",
    )(p, q, ranks, left_factor, right_factor, pivot_sample, right_own, probe_own, *right_plane, *left_line)

    pivot_late, send = lax.optimization_barrier((pivot_left, send))
    left_plane = gather_plane(pivot_late)
    parts = scatter_line(keep, send, F32)
    wide, half = pl.pallas_call(
        samples_kernel,
        out_shape=[jax.ShapeDtypeStruct(share[1:], F32), jax.ShapeDtypeStruct(share[1:], BF)],
        name="samples_sum",
    )(*parts)
    sample_line = gather_line(half)

    basis, keep, send = pl.pallas_call(
        project_kernel(tiles, columns),
        out_shape=[
            jax.ShapeDtypeStruct((span, tiles, rank), F32),
            jax.ShapeDtypeStruct(share, F32),
            jax.ShapeDtypeStruct(share, BF),
        ],
        in_specs=smem(2) + vmem(5 + PIECES + CHIPS * CORES),
        scratch_shapes=[
            pltpu.VMEM((columns, order, rank), BF),
            pltpu.VMEM((tiles, order, rank), BF),
            pltpu.VMEM((tiles, rank, order), BF),
            pltpu.VMEM((tiles, rank, rank), F32),
            pltpu.VMEM((order, rank), F32),
        ],
        name="project",
    )(p, q, left_factor, coupling, target, right_own, wide, *sample_line, *left_plane)
    coefficient = pl.pallas_call(
        finish_kernel,
        out_shape=jax.ShapeDtypeStruct((span, tiles, rank), F32),
        name="finish",
    )(*scatter_line(keep, send, BF))
    return (basis, coefficient)


def solution(mesh):
    in_specs = (
        P("prow", "pcol", None, None),
        P("prow", "pcol", None, None),
        P("pcol", "prow", None),
        P("pcol", "prow", None),
        P("pcol", "prow", None),
        P("pcol", "prow", None),
        P("prow", None),
        P("prow", "pcol"),
    )
    out_specs = (P("pcol", "prow", None), P("pcol", "prow", None))
    return jax.shard_map(
        per_device, mesh=mesh, in_specs=in_specs, out_specs=out_specs, check_vma=False
    )
```

```python
import jax
import jax.numpy as jnp
from jax import lax
from jax.experimental import pallas as pl
from jax.experimental.pallas import tpu as pltpu
from jax.sharding import PartitionSpec as P


HI = lax.Precision.HIGHEST
F32 = jnp.float32
BF = jnp.bfloat16
SIDE = 4
CHIPS = 8
CORES = 2
NB = 32


def dims(a, b, ca, cb, precision=None):
    return lax.dot_general(
        a, b, (((ca,), (cb,)), ((), ())), precision=precision, preferred_element_type=F32
    )


def halves(v):
    high = v.astype(BF)
    return high, (v - high.astype(F32)).astype(BF)


def fine(a, b, ca, cb):
    ah, al = halves(a)
    bh, bl = halves(b)
    return dims(ah, bh, ca, cb) + (dims(ah, bl, ca, cb) + dims(al, bh, ca, cb))


def to_sibling(v):
    return lax.ppermute(v, "pcol", [(i, i ^ 1) for i in range(CHIPS * CORES)])


def along_z(v, k):
    n = CHIPS * CORES
    return lax.ppermute(v, "pcol", [(i, (i + CORES * k) % n) for i in range(n)])


def along_y(v, d):
    return lax.ppermute(
        v, "prow", [(SIDE * x + y, SIDE * x + (y + d) % SIDE) for x in range(SIDE) for y in range(SIDE)]
    )


def along_x(v, d):
    return lax.ppermute(
        v, "prow", [(SIDE * x + y, SIDE * ((x + d) % SIDE) + y) for x in range(SIDE) for y in range(SIDE)]
    )


def first_stage(v, along):
    parts = [along(v, d) for d in (1, 2, -1)]
    return jnp.stack([v, *parts])


def second_stage(stacked, along):
    near = along(stacked, 1)
    far = along(stacked, -1)
    even = along(stacked[:, :1], 2)
    return [stacked, near, even, along(far[:, 1:], -1), far]


def ring(v):
    right, left, up, down = [v], [], v, v
    for step in range(CHIPS // 2):
        up = along_z(up, 1)
        right.append(up)
        if step < CHIPS // 2 - 1:
            down = along_z(down, -1)
            left.insert(0, down)
    return right + left


def ring_loop(v):
    def step(carry, _):
        up, down = carry
        new_up, new_down = along_z(up, 1), along_z(down, -1)
        return (new_up, new_down), (new_up, new_down, to_sibling(up), to_sibling(down))

    (last, _), stacks = lax.scan(step, (v, v), None, length=CHIPS // 2)
    return [v, *stacks, to_sibling(last)]


def scatter_line(keep, send, down_type):
    other = to_sibling(send)
    half = CHIPS // 2

    def share(k):
        return keep[k] + other[k].astype(F32)

    def step(carry, n):
        up, down = carry
        live = n < half - 1
        up = along_z(up, 1).astype(F32) + jnp.where(live, share(half - 1 - n), 0.0)
        down = along_z(down, -1).astype(F32) + jnp.where(live, share((half + 1 + n) % CHIPS), 0.0)
        return (up.astype(BF), down.astype(down_type)), None

    start = (share(half).astype(BF), jnp.zeros(keep.shape[1:], down_type))
    (up, down), _ = lax.scan(step, start, jnp.arange(half))
    return share(0), up, down


def samples_kernel(own, up, down, wide, half):
    acc = own[...] + up[...].astype(F32) + down[...].astype(F32)
    wide[...] = acc
    half[...] = acc.astype(BF)


def finish_kernel(own, up, down, out):
    order = out.shape[0] * CHIPS * CORES
    for i in range(own.shape[0]):
        acc = own[i] + up[i].astype(F32) + down[i].astype(F32)
        out[:, i, :] = acc * (1.0 / order)


def line_rows(q, k, sibling):
    core = q & 1
    chip = ((q >> 1) - k) & (CHIPS - 1)
    return chip * CORES + (core ^ sibling)


def forward_rows(q, k, sibling):
    core = q & 1
    chip = ((q >> 1) + k) & (CHIPS - 1)
    return chip * CORES + (core ^ sibling)


def put_line(q, k, sibling, piece, whole):
    span = piece.shape[1]
    row = pl.multiple_of(line_rows(q, k, sibling) * span, span)
    whole[:, pl.ds(row, span), :] = piece


def place_loop(q, own, up, down, side_up, side_down, side_last, whole):
    half = CHIPS // 2
    put_line(q, 0, 0, own[...], whole)
    put_line(q, half, 1, side_last[...], whole)
    for n in range(half):
        put_line(q, n + 1, 0, up[n], whole)
        put_line(q, n, 1, side_up[n], whole)
        if n < half - 1:
            put_line(q, -n - 1, 0, down[n], whole)
            put_line(q, -n - 1, 1, side_down[n + 1], whole)


def place_plane(p, pieces, swap, whole, start, stop):
    span = pieces[0].shape[2]
    first, near, even, odd, far = pieces
    for piece, d, low, high in [
        (first, 0, 0, None), (near, 1, 0, None), (even, 2, 0, 1), (odd, 2, 1, None), (far, 3, 0, None)
    ]:
        high = low + piece.shape[1] if high is None else high
        lo, hi = max(low, start), min(high, stop)
        if lo >= hi:
            continue
        for e in range(SIDE):
            dx, dy = (e, d) if swap else (d, e)
            x = ((p >> 2) - dx) & (SIDE - 1)
            y = ((p & 3) - dy) & (SIDE - 1)
            row = pl.multiple_of((x * SIDE + y) * span, span)
            whole[lo - start : hi - start, pl.ds(row, span), :] = piece[e, lo - low : hi - low]


def spread(q, i, source, keep, send):
    span = keep.shape[2]
    for k in range(CHIPS):
        row = pl.multiple_of(forward_rows(q, k, 0) * span, span)
        keep[k, i] = source[pl.ds(row, span), :]
        row = pl.multiple_of(forward_rows(q, k, 1) * span, span)
        send[k, i] = source[pl.ds(row, span), :].astype(BF)


PIECES = SIDE + 1


def sample_kernel(tiles, columns):
    def kernel(p_ref, q_ref, ranks, left, right, tright, *refs):
        right_pieces, refs = refs[:PIECES], refs[PIECES:]
        left_pieces, refs = refs[:PIECES], refs[PIECES:]
        line_pieces, refs = refs[:CHIPS], refs[CHIPS:]
        side, coupling, keep, send, whole, lefts, pivot, probe, flip, ps, result = refs
        p, q = p_ref[0], q_ref[0]
        place_plane(p, left_pieces, True, lefts, 0, columns)
        place_plane(p, left_pieces, True, probe, columns, columns + 1)
        for j in range(columns):
            ps[j] = dims(lefts[j].T, probe[0], 1, 0)
        place_plane(p, right_pieces, False, pivot, 0, columns)
        for k, piece in enumerate(line_pieces):
            put_line(q, k, 0, piece[...], whole)
            put_line(q, k, 1, side[k], whole)
        for j in range(columns):
            flip[j] = pivot[j].T
        span = tright.shape[1]
        sketch = probe[0, pl.ds(pl.multiple_of(q * span, span), span), :]

        def tile(i, carry):
            weights = []
            for j in range(columns):
                coup = dims(flip[j], right[i, j], 1, 0).T
                row = lax.broadcasted_iota(jnp.int32, coup.shape, 0)
                coup = jnp.where(row < ranks[i, j], coup, 0.0)
                coupling[i, j] = coup
                weights.append((-fine(coup, ps[j], 1, 0)).astype(BF))
            u = jnp.concatenate([left[i, j] for j in range(columns)], axis=1)
            t = jnp.concatenate([whole[i], whole[i]], axis=1)
            share = jnp.concatenate(halves(dims(tright[i], sketch, 0, 0)), axis=0)
            result[...] = dims(u, jnp.concatenate(weights, axis=0), 1, 0) + dims(t, share, 1, 0)
            spread(q, i, result, keep, send)
            return carry

        lax.fori_loop(0, tiles, tile, 0)

    return kernel


def eliminate(m, width):
    lane = lax.broadcasted_iota(jnp.int32, (8, width), 1)
    sub = lax.broadcasted_iota(jnp.int32, (8, width), 0)
    within = lane & (NB - 1)
    base = lane - within
    for k in range(0, NB, 2):
        b, r = k // 8, k % 8
        at0, at1 = within == k, within == k + 1
        g0 = [jnp.take_along_axis(m[n], base + k, axis=1) if n >= b else None for n in range(len(m))]
        g1 = [jnp.take_along_axis(m[n], base + (k + 1), axis=1) if n >= b else None for n in range(len(m))]
        row0, row1 = m[b][r : r + 1], m[b][r + 1 : r + 2]
        i0 = 1.0 / g0[b][r : r + 1]
        up, low = g1[b][r : r + 1], g0[b][r + 1 : r + 2]
        ratio = up * i0
        i1 = 1.0 / (g1[b][r + 1 : r + 2] - low * ratio)
        at0r, at1r = at0[:1], at1[:1]
        s0 = jnp.where(at0r, i0, row0 * i0)
        next_row = jnp.where(at0r, 0.0, row1) - low * s0
        s1 = jnp.where(at1r, i1, next_row * i1)
        s0 = jnp.where(at1r, 0.0, s0)
        for n in range(b, len(m)):
            new = jnp.where(at0 | at1, 0.0, m[n]) - g0[n] * s0 - (g1[n] - g0[n] * ratio) * s1
            if n == b:
                new = jnp.where(sub > r + 1, new, jnp.where(sub == r + 1, next_row, m[n]))
            m[n] = new
    return m


def factor_inverse(gram):
    tiles, rank, _ = gram.shape
    width = tiles * NB
    lane = lax.broadcasted_iota(jnp.int32, (NB, width), 1)
    row = lax.broadcasted_iota(jnp.int32, (NB, width), 0)
    within = lane & (NB - 1)
    square_row = lax.broadcasted_iota(jnp.int32, (width, width), 0)
    square_lane = lax.broadcasted_iota(jnp.int32, (width, width), 1)
    same = (square_row & -NB) == (square_lane & -NB)
    full_lane = lax.broadcasted_iota(jnp.int32, (rank, rank), 1)
    for start in range(0, rank, NB):
        stop = start + NB
        block = slice(start, stop)
        packed = jnp.concatenate([gram[i, block, block] for i in range(tiles)], axis=1)
        m = eliminate([packed[n : n + 8] for n in range(0, NB, 8)], width)
        m = jnp.concatenate(m, axis=0)
        pivots = jnp.take_along_axis(m, lane - within + row, axis=1)
        unit = jnp.where(within == row, 1.0, jnp.where(within < row, m, 0.0)) / jnp.sqrt(pivots)
        diagonal = jnp.where(same, jnp.concatenate([unit] * tiles, axis=0), 0.0)
        lines = dims(diagonal, jnp.concatenate([gram[i, block, :] for i in range(tiles)], axis=0), 1, 0, HI)
        for i in range(tiles):
            line = lines[i * NB : (i + 1) * NB]
            own = pltpu.roll(unit, (start - i * NB) % width, 1) if (start - i * NB) % width else unit
            inside = (lane >= start) & (lane < stop)
            line = jnp.where(inside, own, line)
            gram[i, block, :] = jnp.where(lane < stop, line, 0.0)
            if stop < rank:
                update = dims(line, line, 0, 0, HI)[stop:]
                rest = gram[i, stop:, :]
                zero = (full_lane[stop:] >= start) & (full_lane[stop:] < stop)
                gram[i, stop:, :] = jnp.where(zero, 0.0, rest) - update


def project_kernel(tiles, columns):
    def kernel(q_ref, left, coupling, target, tright, pivot, wide, *refs):
        line_pieces, refs = refs[:6], refs[6:]
        basis, keep, send, whole, flipped, gram, result = refs
        q = q_ref[0]
        order = whole.shape[1]
        place_loop(q, *line_pieces, whole)

        def square(i, carry):
            flipped[i] = whole[i].T
            gram[i] = dims(flipped[i], whole[i], 1, 0) * (1.0 / order)
            return carry

        lax.fori_loop(0, tiles, square, 0)
        factor_inverse(gram)
        for i in range(tiles):
            basis[:, i, :] = fine(wide[i], gram[i], 1, 1)

        def tile(i, carry):
            inverse = gram[i]
            both = jnp.concatenate([left[i, j] for j in range(columns)], axis=1)
            seen = dims(flipped[i], both, 1, 0)
            span = inverse.shape[1]
            mixed = [
                fine(seen[:, j * span : (j + 1) * span], coupling[i, j], 1, 0) for j in range(columns)
            ]
            mixed.append(dims(flipped[i], target[i], 1, 0))
            solved = fine(inverse, jnp.concatenate(mixed, axis=1), 1, 0).astype(BF)
            u = jnp.concatenate([pivot[j] for j in range(columns)], axis=1)
            result[...] = -dims(u, solved[:, : columns * span], 1, 1)
            spread(q, i, result, keep, send)
            keep[0, i] = keep[0, i] + dims(tright[i], solved[:, columns * span :], 1, 1)
            return carry

        lax.fori_loop(0, tiles, tile, 0)

    return kernel


def vmem(n):
    return [pl.BlockSpec(memory_space=pltpu.VMEM)] * n


def smem(n):
    return [pl.BlockSpec(memory_space=pltpu.SMEM)] * n


def per_device(
    left_factor, right_factor, pivot_left, pivot_right, target_left, target_right, probe, ranks
):
    tiles, columns, order, rank = left_factor.shape
    span = target_left.shape[0]
    p = jnp.full((1,), lax.axis_index("prow"), jnp.int32)
    q = jnp.full((1,), lax.axis_index("pcol"), jnp.int32)
    right_first = first_stage(pivot_right, along_y)
    left_first = first_stage(jnp.concatenate([pivot_left, probe[None]]), along_x)
    line = jnp.transpose(target_left, (1, 0, 2))
    right_plane = second_stage(right_first, along_x)
    left_plane = second_stage(left_first, along_y)
    own_line = ring(line)
    side_line = to_sibling(jnp.stack(own_line))
    right_own = jnp.transpose(target_right, (1, 0, 2))

    share = (CHIPS, tiles, span, rank)
    coupling, keep, send, target, pivot = pl.pallas_call(
        sample_kernel(tiles, columns),
        out_shape=[
            jax.ShapeDtypeStruct((tiles, columns, rank, rank), F32),
            jax.ShapeDtypeStruct(share, F32),
            jax.ShapeDtypeStruct(share, BF),
            jax.ShapeDtypeStruct((tiles, order, rank), BF),
            jax.ShapeDtypeStruct((columns, order, rank), BF),
        ],
        in_specs=smem(3) + vmem(3 + 2 * PIECES + CHIPS + 1),
        scratch_shapes=[
            pltpu.VMEM((columns, order, rank), BF),
            pltpu.VMEM((1, order, rank), BF),
            pltpu.VMEM((columns, rank, order), BF),
            pltpu.VMEM((columns, rank, rank), F32),
            pltpu.VMEM((order, rank), F32),
        ],
        name="sample",
    )(p, q, ranks, left_factor, right_factor, right_own, *right_plane, *left_plane, *own_line, side_line)

    wide, half = pl.pallas_call(
        samples_kernel,
        out_shape=[jax.ShapeDtypeStruct(share[1:], F32), jax.ShapeDtypeStruct(share[1:], BF)],
        name="samples_sum",
    )(*scatter_line(keep, send, F32))

    basis, keep, send = pl.pallas_call(
        project_kernel(tiles, columns),
        out_shape=[
            jax.ShapeDtypeStruct((span, tiles, rank), F32),
            jax.ShapeDtypeStruct(share, F32),
            jax.ShapeDtypeStruct(share, BF),
        ],
        in_specs=smem(1) + vmem(6 + 6),
        scratch_shapes=[
            pltpu.VMEM((tiles, order, rank), BF),
            pltpu.VMEM((tiles, rank, order), BF),
            pltpu.VMEM((tiles, rank, rank), F32),
            pltpu.VMEM((order, rank), F32),
        ],
        name="project",
    )(q, left_factor, coupling, target, right_own, pivot, wide, *ring_loop(half))
    coefficient = pl.pallas_call(
        finish_kernel,
        out_shape=jax.ShapeDtypeStruct((span, tiles, rank), F32),
        name="finish",
    )(*scatter_line(keep, send, BF))
    return (basis, coefficient)


def solution(mesh):
    in_specs = (
        P("prow", "pcol", None, None),
        P("prow", "pcol", None, None),
        P("pcol", "prow", None),
        P("pcol", "prow", None),
        P("pcol", "prow", None),
        P("pcol", "prow", None),
        P("prow", None),
        P("prow", "pcol"),
    )
    out_specs = (P("pcol", "prow", None), P("pcol", "prow", None))

    return jax.shard_map(per_device, mesh=mesh, in_specs=in_specs, out_specs=out_specs, check_vma=False)
```

```python
import jax
import jax.numpy as jnp
from jax import lax
from jax.experimental import pallas as pl
from jax.experimental.pallas import tpu as pltpu
from jax.sharding import PartitionSpec as P


HI = lax.Precision.HIGHEST
F32 = jnp.float32
BF = jnp.bfloat16
SIDE = 4
CHIPS = 8
CORES = 2
NB = 32


def dims(a, b, ca, cb, precision=None):
    return lax.dot_general(
        a, b, (((ca,), (cb,)), ((), ())), precision=precision, preferred_element_type=F32
    )


def halves(v):
    high = v.astype(BF)
    return high, (v - high.astype(F32)).astype(BF)


def fine(a, b, ca, cb):
    ah, al = halves(a)
    bh, bl = halves(b)
    return dims(ah, bh, ca, cb) + (dims(ah, bl, ca, cb) + dims(al, bh, ca, cb))


def to_sibling(v):
    return lax.ppermute(v, "pcol", [(i, i ^ 1) for i in range(CHIPS * CORES)])


def along_z(v, k):
    n = CHIPS * CORES
    return lax.ppermute(v, "pcol", [(i, (i + CORES * k) % n) for i in range(n)])


def along_y(v, d):
    return lax.ppermute(
        v, "prow", [(SIDE * x + y, SIDE * x + (y + d) % SIDE) for x in range(SIDE) for y in range(SIDE)]
    )


def along_x(v, d):
    return lax.ppermute(
        v, "prow", [(SIDE * x + y, SIDE * ((x + d) % SIDE) + y) for x in range(SIDE) for y in range(SIDE)]
    )


def first_stage(v, along):
    return jnp.stack([v, along(v, 1), along(v, 2), along(v, -1)])


def second_stage(stacked, along):
    far, near = along(stacked, -1), along(stacked, 1)
    even = along(stacked[:, :1], 2)
    return [stacked, near, even, along(far[:, 1:], -1), far]


def gather_line(v):
    up = [v]
    down = [v]
    for step in range(CHIPS // 2):
        up.append(along_z(up[-1], 1))
        if step < CHIPS // 2 - 1:
            down.append(along_z(down[-1], -1))
    first = to_sibling(stack(up[0], up[1], up[2], down[1]))
    second = to_sibling(stack(down[2], down[3], up[3], up[4]))
    return up + down[:0:-1] + [first, second]


SIDE_ORDER = ((0, 1, 2, -1), (-2, -3, 3, 4))


def scatter_line(keep, send, down_type):
    other = to_sibling(send)

    def share(k):
        return keep[k] + other[k].astype(F32)

    half = CHIPS // 2
    up, down = share(half).astype(BF), share(half + 1).astype(down_type)
    for k in range(half - 1, 0, -1):
        up = (along_z(up, 1).astype(F32) + share(k)).astype(BF)
        down = along_z(down, -1)
        if k > 1:
            down = (down.astype(F32) + share(CHIPS - k + 1)).astype(down_type)
    return share(0), along_z(up, 1), down


def stack_kernel(*refs):
    out = refs[-1]
    for n, ref in enumerate(refs[:-1]):
        out[n] = ref[...]


def stack(*parts):
    return pl.pallas_call(
        stack_kernel,
        out_shape=jax.ShapeDtypeStruct((len(parts), *parts[0].shape), parts[0].dtype),
        name="stack",
    )(*parts)


def samples_kernel(own, up, down, target, wide, line):
    acc = own[...] + up[...].astype(F32) + down[...].astype(F32)
    span = target.shape[1]
    few = (acc.shape[1] - span) // 2
    wide[...] = acc[:, :span]
    line[:, :span] = acc[:, :span].astype(BF)
    line[:, span : 2 * span] = target[...]
    share = acc[:, span : span + few]
    high = share.astype(BF).astype(F32)
    line[:, 2 * span :] = jnp.concatenate([high, share - high], axis=1).astype(BF)


def finish_kernel(own, up, down, out):
    order = out.shape[0] * CHIPS * CORES
    for i in range(own.shape[0]):
        acc = own[i] + up[i].astype(F32) + down[i].astype(F32)
        out[:, i, :] = acc * (1.0 / order)


def line_rows(q, k, sibling):
    core = q & 1
    chip = ((q >> 1) - k) & (CHIPS - 1)
    return chip * CORES + (core ^ sibling)


def forward_rows(q, k, sibling):
    core = q & 1
    chip = ((q >> 1) + k) & (CHIPS - 1)
    return chip * CORES + (core ^ sibling)


def put_line(q, k, sibling, piece, whole, target, share):
    few = piece.shape[1] // 17 // 2
    span = piece.shape[1] // 17 * 8
    place = line_rows(q, k, sibling)
    row = pl.multiple_of(place * span, span)
    whole[:, pl.ds(row, span), :] = piece[:, :span]
    target[:, pl.ds(row, span), :] = piece[:, span : 2 * span]
    parts = piece[:, 2 * span :].astype(F32)
    share[:, pl.ds(pl.multiple_of(place * few, few), few), :] = parts[:, :few] + parts[:, few:]


def place_plane(p, pieces, swap, whole, start, stop):
    span = pieces[0].shape[2]
    first, near, even, odd, far = pieces
    for piece, d, low, high in [
        (first, 0, 0, None), (near, 1, 0, None), (even, 2, 0, 1), (odd, 2, 1, None), (far, 3, 0, None)
    ]:
        high = low + piece.shape[1] if high is None else high
        lo, hi = max(low, start), min(high, stop)
        if lo >= hi:
            continue
        for e in range(SIDE):
            dx, dy = (e, d) if swap else (d, e)
            x = ((p >> 2) - dx) & (SIDE - 1)
            y = ((p & 3) - dy) & (SIDE - 1)
            row = pl.multiple_of((x * SIDE + y) * span, span)
            whole[lo - start : hi - start, pl.ds(row, span), :] = piece[e, lo - low : hi - low]


def spread(q, i, source, keep, send, share=None):
    span = source.shape[0] // (CHIPS * CORES)
    for k in range(CHIPS):
        for sibling, out, kind in ((0, keep, F32), (1, send, BF)):
            place = forward_rows(q, k, sibling)
            row = pl.multiple_of(place * span, span)
            out[k, i, :span] = source[pl.ds(row, span), :].astype(kind)
            if share is not None:
                few = share.shape[0] // (CHIPS * CORES)
                part = share[pl.ds(pl.multiple_of(place * few, few), few), :]
                out[k, i, span:] = jnp.concatenate([part, jnp.zeros_like(part)], axis=0).astype(kind)


PIECES = SIDE + 1


def sample_kernel(tiles, columns):
    def kernel(p_ref, q_ref, ranks, left_hbm, right_hbm, tright, *refs):
        right_pieces, refs = refs[:PIECES], refs[PIECES:]
        left_pieces, refs = refs[:PIECES], refs[PIECES:]
        coupling, keep, send, lefts, pivot, probe, flip, ps, share, result, left, right, done = refs
        copies = [
            pltpu.make_async_copy(right_hbm, right, done.at[0]),
            pltpu.make_async_copy(left_hbm, left, done.at[1]),
        ]
        for copy in copies:
            copy.start()
        p, q = p_ref[0], q_ref[0]
        place_plane(p, left_pieces, True, lefts, 0, columns)
        place_plane(p, left_pieces, True, probe, columns, columns + 1)
        for j in range(columns):
            ps[j] = dims(lefts[j].T, probe[0], 1, 0)
        place_plane(p, right_pieces, False, pivot, 0, columns)
        for j in range(columns):
            flip[j] = pivot[j].T
        span = tright.shape[1]
        sketch = probe[0, pl.ds(pl.multiple_of(q * span, span), span), :]
        for copy in copies:
            copy.wait()

        def tile(i, carry):
            weights = []
            for j in range(columns):
                coup = dims(flip[j], right[i, j], 1, 0).T
                row = lax.broadcasted_iota(jnp.int32, coup.shape, 0)
                coup = jnp.where(row < ranks[i, j], coup, 0.0)
                coupling[i, j] = coup
                weights.append((-fine(coup, ps[j], 1, 0)).astype(BF))
            u = jnp.concatenate([left[i, j] for j in range(columns)], axis=1)
            share[...] = dims(tright[i], sketch, 0, 0)
            result[...] = dims(u, jnp.concatenate(weights, axis=0), 1, 0)
            spread(q, i, result, keep, send, share)
            return carry

        lax.fori_loop(0, tiles, tile, 0)

    return kernel


def eliminate(m, width):
    lane = lax.broadcasted_iota(jnp.int32, (8, width), 1)
    sub = lax.broadcasted_iota(jnp.int32, (8, width), 0)
    within = lane & (NB - 1)
    base = lane - within
    for k in range(0, NB, 2):
        b, r = k // 8, k % 8
        at0, at1 = within == k, within == k + 1
        g0 = [jnp.take_along_axis(m[n], base + k, axis=1) if n >= b else None for n in range(len(m))]
        g1 = [jnp.take_along_axis(m[n], base + (k + 1), axis=1) if n >= b else None for n in range(len(m))]
        row0, row1 = m[b][r : r + 1], m[b][r + 1 : r + 2]
        i0 = 1.0 / g0[b][r : r + 1]
        up, low = g1[b][r : r + 1], g0[b][r + 1 : r + 2]
        ratio = up * i0
        i1 = 1.0 / (g1[b][r + 1 : r + 2] - low * ratio)
        at0r, at1r = at0[:1], at1[:1]
        s0 = jnp.where(at0r, i0, row0 * i0)
        next_row = jnp.where(at0r, 0.0, row1) - low * s0
        s1 = jnp.where(at1r, i1, next_row * i1)
        s0 = jnp.where(at1r, 0.0, s0)
        for n in range(b, len(m)):
            new = jnp.where(at0 | at1, 0.0, m[n]) - g0[n] * s0 - (g1[n] - g0[n] * ratio) * s1
            if n == b:
                new = jnp.where(sub > r + 1, new, jnp.where(sub == r + 1, next_row, m[n]))
            m[n] = new
    return m


def factor_inverse(gram):
    tiles, rank, _ = gram.shape
    width = tiles * NB
    lane = lax.broadcasted_iota(jnp.int32, (NB, width), 1)
    row = lax.broadcasted_iota(jnp.int32, (NB, width), 0)
    within = lane & (NB - 1)
    square_row = lax.broadcasted_iota(jnp.int32, (width, width), 0)
    square_lane = lax.broadcasted_iota(jnp.int32, (width, width), 1)
    same = (square_row & -NB) == (square_lane & -NB)
    full_lane = lax.broadcasted_iota(jnp.int32, (rank, rank), 1)
    for start in range(0, rank, NB):
        stop = start + NB
        block = slice(start, stop)
        packed = jnp.concatenate([gram[i, block, block] for i in range(tiles)], axis=1)
        m = eliminate([packed[n : n + 8] for n in range(0, NB, 8)], width)
        m = jnp.concatenate(m, axis=0)
        pivots = jnp.take_along_axis(m, lane - within + row, axis=1)
        unit = jnp.where(within == row, 1.0, jnp.where(within < row, m, 0.0)) / jnp.sqrt(pivots)
        diagonal = jnp.where(same, jnp.concatenate([unit] * tiles, axis=0), 0.0)
        lines = dims(diagonal, jnp.concatenate([gram[i, block, :] for i in range(tiles)], axis=0), 1, 0, HI)
        for i in range(tiles):
            line = lines[i * NB : (i + 1) * NB]
            own = pltpu.roll(unit, (start - i * NB) % width, 1) if (start - i * NB) % width else unit
            inside = (lane >= start) & (lane < stop)
            line = jnp.where(inside, own, line)
            gram[i, block, :] = jnp.where(lane < stop, line, 0.0)
            if stop < rank:
                update = dims(line, line, 0, 0, HI)[stop:]
                rest = gram[i, stop:, :]
                zero = (full_lane[stop:] >= start) & (full_lane[stop:] < stop)
                gram[i, stop:, :] = jnp.where(zero, 0.0, rest) - update


def project_kernel(tiles, columns):
    def kernel(q_ref, left_hbm, coupling, tright, pivot, wide, *refs):
        line_pieces, refs = refs[:CHIPS], refs[CHIPS:]
        side_pieces, refs = refs[:2], refs[2:]
        basis, keep, send, whole, target, share, exact, flipped, gram, result, left, done = refs
        copy = pltpu.make_async_copy(left_hbm, left, done)
        copy.start()
        q = q_ref[0]
        order = whole.shape[1]
        own = pl.ds(pl.multiple_of(q * wide.shape[1], wide.shape[1]), wide.shape[1])
        for k, piece in enumerate(line_pieces):
            put_line(q, k, 0, piece[...], whole, target, share)
        for piece, ks in zip(side_pieces, SIDE_ORDER):
            for n, k in enumerate(ks):
                put_line(q, k, 1, piece[n], whole, target, share)

        def square(i, carry):
            both = jnp.concatenate(halves(share[i]), axis=0)
            t = jnp.concatenate([target[i], target[i]], axis=1)
            term = dims(t, both, 1, 0)
            result[...] = term
            exact[i] = wide[i] + result[own, :]
            whole[i] = (whole[i].astype(F32) + term).astype(BF)
            flipped[i] = whole[i].T
            gram[i] = dims(flipped[i], whole[i], 1, 0) * (1.0 / order)
            return carry

        lax.fori_loop(0, tiles, square, 0)
        copy.wait()
        factor_inverse(gram)
        for i in range(tiles):
            basis[:, i, :] = fine(exact[i], gram[i], 1, 1)

        def tile(i, carry):
            inverse = gram[i]
            both = jnp.concatenate([left[i, j] for j in range(columns)], axis=1)
            seen = dims(flipped[i], both, 1, 0)
            span = inverse.shape[1]
            mixed = [
                fine(seen[:, j * span : (j + 1) * span], coupling[i, j], 1, 0) for j in range(columns)
            ]
            mixed.append(dims(flipped[i], target[i], 1, 0))
            solved = fine(inverse, jnp.concatenate(mixed, axis=1), 1, 0).astype(BF)
            u = jnp.concatenate([pivot[j] for j in range(columns)], axis=1)
            result[...] = -dims(u, solved[:, : columns * span], 1, 1)
            spread(q, i, result, keep, send)
            keep[0, i] = keep[0, i] + dims(tright[i], solved[:, columns * span :], 1, 1)
            return carry

        lax.fori_loop(0, tiles, tile, 0)

    return kernel


def vmem(n):
    return [pl.BlockSpec(memory_space=pltpu.VMEM)] * n


def anywhere(n):
    return [pl.BlockSpec(memory_space=pl.ANY)] * n


def smem(n):
    return [pl.BlockSpec(memory_space=pltpu.SMEM)] * n


def per_device(
    left_factor, right_factor, pivot_left, pivot_right, target_left, target_right, probe, ranks
):
    tiles, columns, order, rank = left_factor.shape
    span = target_left.shape[0]
    n_col = CHIPS * CORES
    p = jnp.full((1,), lax.axis_index("prow"), jnp.int32)
    q = jnp.full((1,), lax.axis_index("pcol"), jnp.int32)
    right_first = first_stage(pivot_right, along_y)
    left_first = first_stage(jnp.concatenate([pivot_left, probe[None]]), along_x)
    right_plane = second_stage(right_first, along_x)
    left_plane = second_stage(left_first, along_y)
    left_own = jnp.transpose(target_left, (1, 0, 2))
    right_own = jnp.transpose(target_right, (1, 0, 2))

    few = 2 * rank // n_col
    tall = (CHIPS, tiles, span + few, rank)
    coupling, keep, send, pivot = pl.pallas_call(
        sample_kernel(tiles, columns),
        out_shape=[
            jax.ShapeDtypeStruct((tiles, columns, rank, rank), F32),
            jax.ShapeDtypeStruct(tall, F32),
            jax.ShapeDtypeStruct(tall, BF),
            jax.ShapeDtypeStruct((columns, order, rank), BF),
        ],
        in_specs=smem(3) + anywhere(2) + vmem(1 + 2 * PIECES),
        scratch_shapes=[
            pltpu.VMEM((columns, order, rank), BF),
            pltpu.VMEM((1, order, rank), BF),
            pltpu.VMEM((columns, rank, order), BF),
            pltpu.VMEM((columns, rank, rank), F32),
            pltpu.VMEM((rank, rank), F32),
            pltpu.VMEM((order, rank), F32),
            pltpu.VMEM(left_factor.shape, BF),
            pltpu.VMEM(left_factor.shape, BF),
            pltpu.SemaphoreType.DMA((2,)),
        ],
        name="sample",
    )(p, q, ranks, left_factor, right_factor, right_own, *right_plane, *left_plane)

    wide, line = pl.pallas_call(
        samples_kernel,
        out_shape=[
            jax.ShapeDtypeStruct((tiles, span, rank), F32),
            jax.ShapeDtypeStruct((tiles, 2 * span + few, rank), BF),
        ],
        name="samples_sum",
    )(*scatter_line(keep, send, F32), left_own)

    share = (CHIPS, tiles, span, rank)
    basis, keep, send = pl.pallas_call(
        project_kernel(tiles, columns),
        out_shape=[
            jax.ShapeDtypeStruct((span, tiles, rank), F32),
            jax.ShapeDtypeStruct(share, F32),
            jax.ShapeDtypeStruct(share, BF),
        ],
        in_specs=smem(1) + anywhere(1) + vmem(4 + CHIPS + 2),
        scratch_shapes=[
            pltpu.VMEM((tiles, order, rank), BF),
            pltpu.VMEM((tiles, order, rank), BF),
            pltpu.VMEM((tiles, rank, rank), F32),
            pltpu.VMEM((tiles, span, rank), F32),
            pltpu.VMEM((tiles, rank, order), BF),
            pltpu.VMEM((tiles, rank, rank), F32),
            pltpu.VMEM((order, rank), F32),
            pltpu.VMEM(left_factor.shape, BF),
            pltpu.SemaphoreType.DMA,
        ],
        name="project",
    )(q, left_factor, coupling, right_own, pivot, wide, *gather_line(line))
    coefficient = pl.pallas_call(
        finish_kernel,
        out_shape=jax.ShapeDtypeStruct((span, tiles, rank), F32),
        name="finish",
    )(*scatter_line(keep, send, BF))
    return (basis, coefficient)


def solution(mesh):
    in_specs = (
        P("prow", "pcol", None, None),
        P("prow", "pcol", None, None),
        P("pcol", "prow", None),
        P("pcol", "prow", None),
        P("pcol", "prow", None),
        P("pcol", "prow", None),
        P("prow", None),
        P("prow", "pcol"),
    )
    out_specs = (P("pcol", "prow", None), P("pcol", "prow", None))
    return jax.shard_map(
        per_device, mesh=mesh, in_specs=in_specs, out_specs=out_specs, check_vma=False
    )
```

```python
import jax
import jax.numpy as jnp
from jax import lax
from jax.experimental import pallas as pl
from jax.experimental.pallas import tpu as pltpu
from jax.sharding import PartitionSpec as P


F32 = jnp.float32
BF = jnp.bfloat16
SIDE = 4
CHIPS = 8
CORES = 2
NB = 32


def dims(a, b, ca, cb, precision=None):
    return lax.dot_general(
        a, b, (((ca,), (cb,)), ((), ())), precision=precision, preferred_element_type=F32
    )


def halves(v):
    high = v.astype(BF)
    return high, (v - high.astype(F32)).astype(BF)


def fine(a, b, ca, cb):
    ah, al = halves(a)
    bh, bl = halves(b)
    return dims(ah, bh, ca, cb) + (dims(ah, bl, ca, cb) + dims(al, bh, ca, cb))


def to_sibling(v):
    return lax.ppermute(v, "pcol", [(i, i ^ 1) for i in range(CHIPS * CORES)])


def along_z(v, k):
    n = CHIPS * CORES
    return lax.ppermute(v, "pcol", [(i, (i + CORES * k) % n) for i in range(n)])


def along_y(v, d):
    return lax.ppermute(
        v, "prow", [(SIDE * x + y, SIDE * x + (y + d) % SIDE) for x in range(SIDE) for y in range(SIDE)]
    )


def along_x(v, d):
    return lax.ppermute(
        v, "prow", [(SIDE * x + y, SIDE * ((x + d) % SIDE) + y) for x in range(SIDE) for y in range(SIDE)]
    )


def first_stage(v, along):
    parts = [along(v, d) for d in (1, 2, -1)]
    return jnp.stack([v, *parts])


def second_stage(stacked, along, tag):
    far = along(stacked, -1)
    near = along(stacked, 1)
    if tag == "rights":
        return [stacked, near, along(stacked, 2), far]
    even = along(stacked[:, :1], 2)
    return [stacked, near, even, along(far[:, 1:], -1), far]


def gather_line(v):
    up = [v]
    down = [v]
    for step in range(CHIPS // 2):
        up.append(along_z(up[-1], 1))
        if step < CHIPS // 2 - 1:
            down.append(along_z(down[-1], -1))
    first = to_sibling(stack(up[0], up[1], up[2], down[1]))
    second = to_sibling(stack(down[2], down[3], up[3], up[4]))
    return up + down[:0:-1] + [first, second]


SIDE_ORDER = ((0, 1, 2, -1), (-2, -3, 3, 4))


def scatter_line(keep, send, down_type, few):
    other = to_sibling(send)
    half = CHIPS // 2
    up, down, own = begin(keep, other, few, down_type)
    for k in range(half - 1, 0, -1):
        up = onward(along_z(up, 1), keep, other, k, few)
        down = along_z(down, -1)
        if k > 1:
            share = keep[CHIPS - k + 1] + other[CHIPS - k + 1].astype(F32)
            down = (down.astype(F32) + share).astype(down_type)
    return own, along_z(up, 1), down


def narrow(out, value, few):
    if not few:
        out[...] = value.astype(BF)
        return
    span = value.shape[1] - 2 * few
    out[:, :span] = value[:, :span].astype(BF)
    whole = value[:, span : span + few] + value[:, span + few :]
    high = whole.astype(BF).astype(F32)
    out[:, span:] = jnp.concatenate([high, whole - high], axis=1).astype(BF)


def block(shape, k):
    return pl.BlockSpec((1, *shape), lambda _: (k, *[0] * len(shape)))


def begin(keep, other, few, down_type):
    shape = keep.shape[1:]
    half = CHIPS // 2

    def kernel(k0, k1, k2, o0, o1, o2, up, down, own):
        narrow(up, k0[0] + o0[0].astype(F32), few)
        down[...] = (k1[0] + o1[0].astype(F32)).astype(down_type)
        own[...] = k2[0] + o2[0].astype(F32)

    blocks = [block(shape, k) for k in (half, half + 1, 0)]
    return pl.pallas_call(
        kernel,
        grid=(1,),
        in_specs=blocks + blocks,
        out_specs=[pl.BlockSpec(shape, lambda _: (0,) * len(shape))] * 3,
        out_shape=[jax.ShapeDtypeStruct(shape, t) for t in (BF, down_type, F32)],
        name="begin",
    )(keep, keep, keep, other, other, other)


def onward(got, keep, other, k, few):
    shape = keep.shape[1:]
    plain = pl.BlockSpec(shape, lambda _: (0,) * len(shape))

    def kernel(g, k0, o0, out):
        narrow(out, g[...].astype(F32) + k0[0] + o0[0].astype(F32), few)

    return pl.pallas_call(
        kernel,
        grid=(1,),
        in_specs=[plain, block(shape, k), block(shape, k)],
        out_specs=plain,
        out_shape=jax.ShapeDtypeStruct(shape, BF),
        name="onward",
    )(got, keep, other)


def stack_kernel(*refs):
    out = refs[-1]
    for n, ref in enumerate(refs[:-1]):
        out[n] = ref[...]


def stack(*parts):
    return pl.pallas_call(
        stack_kernel,
        out_shape=jax.ShapeDtypeStruct((len(parts), *parts[0].shape), parts[0].dtype),
        name="stack",
    )(*parts)


def samples_kernel(own, up, down, target, wide, line):
    acc = own[...] + up[...].astype(F32) + down[...].astype(F32)
    span = target.shape[1]
    few = (acc.shape[1] - span) // 2
    wide[...] = acc[:, :span]
    line[:, :span] = acc[:, :span].astype(BF)
    line[:, span : 2 * span] = target[...]
    share = acc[:, span : span + few] + acc[:, span + few :]
    high = share.astype(BF).astype(F32)
    line[:, 2 * span :] = jnp.concatenate([high, share - high], axis=1).astype(BF)


def finish_kernel(own, up, down, out):
    order = out.shape[0] * CHIPS * CORES
    for i in range(own.shape[0]):
        acc = own[i] + up[i].astype(F32) + down[i].astype(F32)
        out[:, i, :] = acc * (1.0 / order)


def line_rows(q, k, sibling):
    core = q & 1
    chip = ((q >> 1) - k) & (CHIPS - 1)
    return chip * CORES + (core ^ sibling)


def forward_rows(q, k, sibling):
    core = q & 1
    chip = ((q >> 1) + k) & (CHIPS - 1)
    return chip * CORES + (core ^ sibling)


def put_line(q, k, sibling, piece, whole, target, share):
    few = piece.shape[1] // 17 // 2
    span = piece.shape[1] // 17 * 8
    place = line_rows(q, k, sibling)
    row = pl.multiple_of(place * span, span)
    whole[:, pl.ds(row, span), :] = piece[:, :span]
    target[:, pl.ds(row, span), :] = piece[:, span : 2 * span]
    parts = piece[:, 2 * span :].astype(F32)
    share[:, pl.ds(pl.multiple_of(place * few, few), few), :] = parts[:, :few] + parts[:, few:]


def place_plane(p, pieces, swap, whole, start, stop):
    span = pieces[0].shape[2]
    if len(pieces) == SIDE:
        parts = [(piece, d, 0) for d, piece in enumerate(pieces)]
    else:
        first, near, even, odd, far = pieces
        parts = [(first, 0, 0), (near, 1, 0), (even, 2, 0), (odd, 2, 1), (far, 3, 0)]
    for piece, d, low in parts:
        lo, hi = max(low, start), min(low + piece.shape[1], stop)
        if lo >= hi:
            continue
        for e in range(SIDE):
            dx, dy = (e, d) if swap else (d, e)
            x = ((p >> 2) - dx) & (SIDE - 1)
            y = ((p & 3) - dy) & (SIDE - 1)
            row = pl.multiple_of((x * SIDE + y) * span, span)
            whole[lo - start : hi - start, pl.ds(row, span), :] = piece[e, lo - low : hi - low]


def spread(q, i, source, keep, send, share=None):
    span = source.shape[0] // (CHIPS * CORES)
    for k in range(CHIPS):
        for sibling, out, kind in ((0, keep, F32), (1, send, BF)):
            place = forward_rows(q, k, sibling)
            row = pl.multiple_of(place * span, span)
            out[k, i, :span] = source[pl.ds(row, span), :].astype(kind)
            if share is not None:
                few = share.shape[0] // (CHIPS * CORES)
                part = share[pl.ds(pl.multiple_of(place * few, few), few), :]
                high = part if kind == F32 else part.astype(BF).astype(F32)
                out[k, i, span:] = jnp.concatenate([high, part - high], axis=0).astype(kind)


PIECES = SIDE + 1


def sample_kernel(tiles, columns):
    def kernel(p_ref, q_ref, ranks, left_hbm, right_hbm, tright, *refs):
        right_pieces, refs = refs[:SIDE], refs[SIDE:]
        left_pieces, refs = refs[:PIECES], refs[PIECES:]
        coupling, keep, send, lefts, pivot, probe, flip, ps, share, result, left, right, done = refs
        copies = [
            pltpu.make_async_copy(right_hbm, right, done.at[0]),
            pltpu.make_async_copy(left_hbm, left, done.at[1]),
        ]
        for copy in copies:
            copy.start()
        p, q = p_ref[0], q_ref[0]
        place_plane(p, left_pieces, True, lefts, 0, columns)
        place_plane(p, left_pieces, True, probe, columns, columns + 1)
        for j in range(columns):
            ps[j] = dims(lefts[j].T, probe[0], 1, 0)
        place_plane(p, right_pieces, False, pivot, 0, columns)
        for j in range(columns):
            flip[j] = pivot[j].T
        span = tright.shape[1]
        sketch = probe[0, pl.ds(pl.multiple_of(q * span, span), span), :]
        for copy in copies:
            copy.wait()

        def tile(i, carry):
            weights = []
            for j in range(columns):
                coup = dims(flip[j], right[i, j], 1, 0).T
                row = lax.broadcasted_iota(jnp.int32, coup.shape, 0)
                coup = jnp.where(row < ranks[i, j], coup, 0.0)
                coupling[i, j] = coup
                weights.append((-fine(coup, ps[j], 1, 0)).astype(BF))
            u = jnp.concatenate([left[i, j] for j in range(columns)], axis=1)
            share[...] = dims(tright[i], sketch, 0, 0)
            result[...] = dims(u, jnp.concatenate(weights, axis=0), 1, 0)
            spread(q, i, result, keep, send, share)
            return carry

        lax.fori_loop(0, tiles, tile, 0)

    return kernel


def eliminate(m, width):
    lane = lax.broadcasted_iota(jnp.int32, (8, width), 1)
    sub = lax.broadcasted_iota(jnp.int32, (8, width), 0)
    within = lane & (NB - 1)
    base = lane - within
    for k in range(0, NB, 2):
        b, r = k // 8, k % 8
        at0, at1 = within == k, within == k + 1
        g0 = [jnp.take_along_axis(m[n], base + k, axis=1) if n >= b else None for n in range(len(m))]
        g1 = [jnp.take_along_axis(m[n], base + (k + 1), axis=1) if n >= b else None for n in range(len(m))]
        row0, row1 = m[b][r : r + 1], m[b][r + 1 : r + 2]
        i0 = 1.0 / g0[b][r : r + 1]
        up, low = g1[b][r : r + 1], g0[b][r + 1 : r + 2]
        ratio = up * i0
        i1 = 1.0 / (g1[b][r + 1 : r + 2] - low * ratio)
        at0r, at1r = at0[:1], at1[:1]
        s0 = jnp.where(at0r, i0, row0 * i0)
        next_row = jnp.where(at0r, 0.0, row1) - low * s0
        s1 = jnp.where(at1r, i1, next_row * i1)
        s0 = jnp.where(at1r, 0.0, s0)
        for n in range(b, len(m)):
            new = jnp.where(at0 | at1, 0.0, m[n]) - g0[n] * s0 - (g1[n] - g0[n] * ratio) * s1
            if n == b:
                new = jnp.where(sub > r + 1, new, jnp.where(sub == r + 1, next_row, m[n]))
            m[n] = new
    return m


def factor_inverse(gram):
    tiles, rank, _ = gram.shape
    width = tiles * NB
    lane = lax.broadcasted_iota(jnp.int32, (NB, width), 1)
    row = lax.broadcasted_iota(jnp.int32, (NB, width), 0)
    within = lane & (NB - 1)
    square_row = lax.broadcasted_iota(jnp.int32, (width, width), 0)
    square_lane = lax.broadcasted_iota(jnp.int32, (width, width), 1)
    same = (square_row & -NB) == (square_lane & -NB)
    full_lane = lax.broadcasted_iota(jnp.int32, (rank, rank), 1)
    for start in range(0, rank, NB):
        stop = start + NB
        block = slice(start, stop)
        packed = jnp.concatenate([gram[i, block, block] for i in range(tiles)], axis=1)
        m = eliminate([packed[n : n + 8] for n in range(0, NB, 8)], width)
        m = jnp.concatenate(m, axis=0)
        pivots = jnp.take_along_axis(m, lane - within + row, axis=1)
        unit = jnp.where(within == row, 1.0, jnp.where(within < row, m, 0.0)) / jnp.sqrt(pivots)
        diagonal = jnp.where(same, jnp.concatenate([unit] * tiles, axis=0), 0.0)
        lines = fine(diagonal, jnp.concatenate([gram[i, block, :] for i in range(tiles)], axis=0), 1, 0)
        for i in range(tiles):
            line = lines[i * NB : (i + 1) * NB]
            own = pltpu.roll(unit, (start - i * NB) % width, 1) if (start - i * NB) % width else unit
            inside = (lane >= start) & (lane < stop)
            line = jnp.where(inside, own, line)
            gram[i, block, :] = jnp.where(lane < stop, line, 0.0)
            if stop < rank:
                update = fine(line, line, 0, 0)[stop:]
                rest = gram[i, stop:, :]
                zero = (full_lane[stop:] >= start) & (full_lane[stop:] < stop)
                gram[i, stop:, :] = jnp.where(zero, 0.0, rest) - update


def project_kernel(tiles, columns):
    def kernel(q_ref, left_hbm, coupling, tright, pivot, wide, *refs):
        line_pieces, refs = refs[:CHIPS], refs[CHIPS:]
        side_pieces, refs = refs[:2], refs[2:]
        exact, gram, keep, send, whole, target, share, flipped, result, left, done = refs
        copy = pltpu.make_async_copy(left_hbm, left, done)
        copy.start()
        q = q_ref[0]
        order = whole.shape[1]
        own = pl.ds(pl.multiple_of(q * wide.shape[1], wide.shape[1]), wide.shape[1])
        for k, piece in enumerate(line_pieces):
            put_line(q, k, 0, piece[...], whole, target, share)
        for piece, ks in zip(side_pieces, SIDE_ORDER):
            for n, k in enumerate(ks):
                put_line(q, k, 1, piece[n], whole, target, share)

        def square(i, carry):
            both = jnp.concatenate(halves(share[i]), axis=0)
            t = jnp.concatenate([target[i], target[i]], axis=1)
            term = dims(t, both, 1, 0)
            result[...] = term
            exact[i] = wide[i] + result[own, :]
            whole[i] = (whole[i].astype(F32) + term).astype(BF)
            flipped[i] = whole[i].T
            gram[i] = dims(flipped[i], whole[i], 1, 0) * (1.0 / order)
            return carry

        lax.fori_loop(0, tiles, square, 0)
        copy.wait()
        factor_inverse(gram)

        def tile(i, carry):
            inverse = gram[i]
            both = jnp.concatenate([left[i, j] for j in range(columns)], axis=1)
            seen = dims(flipped[i], both, 1, 0)
            span = inverse.shape[1]
            mixed = [
                fine(seen[:, j * span : (j + 1) * span], coupling[i, j], 1, 0) for j in range(columns)
            ]
            mixed.append(dims(flipped[i], target[i], 1, 0))
            solved = fine(inverse, jnp.concatenate(mixed, axis=1), 1, 0).astype(BF)
            u = jnp.concatenate([pivot[j] for j in range(columns)], axis=1)
            result[...] = -dims(u, solved[:, : columns * span], 1, 1)
            spread(q, i, result, keep, send)
            keep[0, i] = keep[0, i] + dims(tright[i], solved[:, columns * span :], 1, 1)
            return carry

        lax.fori_loop(0, tiles, tile, 0)

    return kernel


def vmem(n):
    return [pl.BlockSpec(memory_space=pltpu.VMEM)] * n


def basis_kernel(exact, inverse, out):
    for i in range(exact.shape[0]):
        out[:, i, :] = fine(exact[i], inverse[i], 1, 1)


def anywhere(n):
    return [pl.BlockSpec(memory_space=pl.ANY)] * n


def smem(n):
    return [pl.BlockSpec(memory_space=pltpu.SMEM)] * n


def per_device(
    left_factor, right_factor, pivot_left, pivot_right, target_left, target_right, probe, ranks
):
    tiles, columns, order, rank = left_factor.shape
    span = target_left.shape[0]
    n_col = CHIPS * CORES
    p = jnp.full((1,), lax.axis_index("prow"), jnp.int32)
    q = jnp.full((1,), lax.axis_index("pcol"), jnp.int32)
    right_first = first_stage(pivot_right, along_y)
    left_first = first_stage(jnp.concatenate([pivot_left, probe[None]]), along_x)
    right_plane = second_stage(right_first, along_x, "rights")
    left_plane = second_stage(left_first, along_y, "lefts")
    left_own = jnp.transpose(target_left, (1, 0, 2))
    right_own = jnp.transpose(target_right, (1, 0, 2))

    few = 2 * rank // n_col
    tall = (CHIPS, tiles, span + few, rank)
    coupling, keep, send, pivot = pl.pallas_call(
        sample_kernel(tiles, columns),
        out_shape=[
            jax.ShapeDtypeStruct((tiles, columns, rank, rank), F32),
            jax.ShapeDtypeStruct(tall, F32),
            jax.ShapeDtypeStruct(tall, BF),
            jax.ShapeDtypeStruct((columns, order, rank), BF),
        ],
        in_specs=smem(3) + anywhere(2) + vmem(1 + SIDE + PIECES),
        scratch_shapes=[
            pltpu.VMEM((columns, order, rank), BF),
            pltpu.VMEM((1, order, rank), BF),
            pltpu.VMEM((columns, rank, order), BF),
            pltpu.VMEM((columns, rank, rank), F32),
            pltpu.VMEM((rank, rank), F32),
            pltpu.VMEM((order, rank), F32),
            pltpu.VMEM(left_factor.shape, BF),
            pltpu.VMEM(left_factor.shape, BF),
            pltpu.SemaphoreType.DMA((2,)),
        ],
        name="sample",
    )(p, q, ranks, left_factor, right_factor, right_own, *right_plane, *left_plane)

    wide, line = pl.pallas_call(
        samples_kernel,
        out_shape=[
            jax.ShapeDtypeStruct((tiles, span, rank), F32),
            jax.ShapeDtypeStruct((tiles, 2 * span + few, rank), BF),
        ],
        name="samples_sum",
    )(*scatter_line(keep, send, F32, few // 2), left_own)

    share = (CHIPS, tiles, span, rank)
    exact, inverse, keep, send = pl.pallas_call(
        project_kernel(tiles, columns),
        out_shape=[
            jax.ShapeDtypeStruct((tiles, span, rank), F32),
            jax.ShapeDtypeStruct((tiles, rank, rank), F32),
            jax.ShapeDtypeStruct(share, F32),
            jax.ShapeDtypeStruct(share, BF),
        ],
        in_specs=smem(1) + anywhere(1) + vmem(4 + CHIPS + 2),
        scratch_shapes=[
            pltpu.VMEM((tiles, order, rank), BF),
            pltpu.VMEM((tiles, order, rank), BF),
            pltpu.VMEM((tiles, rank, rank), F32),
            pltpu.VMEM((tiles, rank, order), BF),
            pltpu.VMEM((order, rank), F32),
            pltpu.VMEM(left_factor.shape, BF),
            pltpu.SemaphoreType.DMA,
        ],
        name="project",
    )(q, left_factor, coupling, right_own, pivot, wide, *gather_line(line))
    basis = pl.pallas_call(
        basis_kernel, out_shape=jax.ShapeDtypeStruct((span, tiles, rank), F32), name="basis"
    )(exact, inverse)
    coefficient = pl.pallas_call(
        finish_kernel,
        out_shape=jax.ShapeDtypeStruct((span, tiles, rank), F32),
        name="finish",
    )(*scatter_line(keep, send, BF, 0))
    return (basis, coefficient)


def solution(mesh):
    in_specs = (
        P("prow", "pcol", None, None),
        P("prow", "pcol", None, None),
        P("pcol", "prow", None),
        P("pcol", "prow", None),
        P("pcol", "prow", None),
        P("pcol", "prow", None),
        P("prow", None),
        P("prow", "pcol"),
    )
    out_specs = (P("pcol", "prow", None), P("pcol", "prow", None))

    return jax.shard_map(per_device, mesh=mesh, in_specs=in_specs, out_specs=out_specs, check_vma=False)
```

```python
import jax
import jax.numpy as jnp
from jax import lax
from jax.experimental import pallas as pl
from jax.experimental.pallas import tpu as pltpu
from jax.sharding import PartitionSpec as P


F32 = jnp.float32
BF = jnp.bfloat16
SIDE = 4
CHIPS = 8
CORES = 2
NB = 32


def dims(a, b, ca, cb, precision=None):
    return lax.dot_general(
        a, b, (((ca,), (cb,)), ((), ())), precision=precision, preferred_element_type=F32
    )


def halves(v):
    high = v.astype(BF)
    return high, (v - high.astype(F32)).astype(BF)


def fine(a, b, ca, cb):
    ah, al = halves(a)
    bh, bl = halves(b)
    return dims(ah, bh, ca, cb) + (dims(ah, bl, ca, cb) + dims(al, bh, ca, cb))


def to_sibling(v):
    return lax.ppermute(v, "pcol", [(i, i ^ 1) for i in range(CHIPS * CORES)])


def along_z(v, k):
    n = CHIPS * CORES
    return lax.ppermute(v, "pcol", [(i, (i + CORES * k) % n) for i in range(n)])


def along_y(v, d):
    return lax.ppermute(
        v, "prow", [(SIDE * x + y, SIDE * x + (y + d) % SIDE) for x in range(SIDE) for y in range(SIDE)]
    )


def along_x(v, d):
    return lax.ppermute(
        v, "prow", [(SIDE * x + y, SIDE * ((x + d) % SIDE) + y) for x in range(SIDE) for y in range(SIDE)]
    )


def first_stage(v, along):
    parts = [along(v, d) for d in (1, 2, -1)]
    return jnp.stack([v, *parts])


def second_stage(stacked, along, tag):
    far = along(stacked, -1)
    near = along(stacked, 1)
    if tag == "rights":
        return [stacked, near, along(stacked, 2), far]
    even = along(stacked[:, :1], 2)
    return [stacked, near, even, along(far[:, 1:], -1), far]


def gather_line(v):
    up = [v]
    down = [v]
    for step in range(CHIPS // 2):
        up.append(along_z(up[-1], 1))
        if step < CHIPS // 2 - 1:
            down.append(along_z(down[-1], -1))
    first = to_sibling(stack(up[0], up[1], up[2], down[1]))
    second = to_sibling(stack(down[2], down[3], up[3]))
    return up + down[:0:-1] + [first, second, to_sibling(up[4][None])]


SIDE_ORDER = ((0, 1, 2, -1), (-2, -3, 3), (4,))


def scatter_line(keep, send, down_type, few):
    other = to_sibling(send)
    half = CHIPS // 2

    def share(k):
        return keep[k] + other[k].astype(F32)

    if few:
        up, down, own = begin(keep, other, few, down_type)
    else:
        up, down, own = share(half).astype(BF), share(half + 1).astype(down_type), share(0)
    for k in range(half - 1, 0, -1):
        up = along_z(up, 1)
        up = onward(up, keep, other, k, few) if few else (up.astype(F32) + share(k)).astype(BF)
        down = along_z(down, -1)
        if k > 1:
            down = (down.astype(F32) + share(CHIPS - k + 1)).astype(down_type)
    return own, along_z(up, 1), down


def narrow(out, value, few):
    if not few:
        out[...] = value.astype(BF)
        return
    span = value.shape[1] - 2 * few
    out[:, :span] = value[:, :span].astype(BF)
    whole = value[:, span : span + few] + value[:, span + few :]
    high = whole.astype(BF).astype(F32)
    out[:, span:] = jnp.concatenate([high, whole - high], axis=1).astype(BF)


def block(shape, k):
    return pl.BlockSpec((1, *shape), lambda _: (k, *[0] * len(shape)))


def begin(keep, other, few, down_type):
    shape = keep.shape[1:]
    half = CHIPS // 2

    def kernel(k0, k1, k2, o0, o1, o2, up, down, own):
        narrow(up, k0[0] + o0[0].astype(F32), few)
        down[...] = (k1[0] + o1[0].astype(F32)).astype(down_type)
        own[...] = k2[0] + o2[0].astype(F32)

    blocks = [block(shape, k) for k in (half, half + 1, 0)]
    return pl.pallas_call(
        kernel,
        grid=(1,),
        in_specs=blocks + blocks,
        out_specs=[pl.BlockSpec(shape, lambda _: (0,) * len(shape))] * 3,
        out_shape=[jax.ShapeDtypeStruct(shape, t) for t in (BF, down_type, F32)],
        name="begin",
    )(keep, keep, keep, other, other, other)


def onward(got, keep, other, k, few):
    shape = keep.shape[1:]
    plain = pl.BlockSpec(shape, lambda _: (0,) * len(shape))

    def kernel(g, k0, o0, out):
        narrow(out, g[...].astype(F32) + k0[0] + o0[0].astype(F32), few)

    return pl.pallas_call(
        kernel,
        grid=(1,),
        in_specs=[plain, block(shape, k), block(shape, k)],
        out_specs=plain,
        out_shape=jax.ShapeDtypeStruct(shape, BF),
        name="onward",
    )(got, keep, other)


def stack_kernel(*refs):
    out = refs[-1]
    for n, ref in enumerate(refs[:-1]):
        out[n] = ref[...]


def stack(*parts):
    return pl.pallas_call(
        stack_kernel,
        out_shape=jax.ShapeDtypeStruct((len(parts), *parts[0].shape), parts[0].dtype),
        name="stack",
    )(*parts)


def samples_kernel(own, up, down, target, wide, line):
    acc = own[...] + up[...].astype(F32) + down[...].astype(F32)
    span = target.shape[1]
    few = (acc.shape[1] - span) // 2
    wide[...] = acc[:, :span]
    line[:, :span] = acc[:, :span].astype(BF)
    line[:, span : 2 * span] = target[...]
    share = acc[:, span : span + few] + acc[:, span + few :]
    high = share.astype(BF).astype(F32)
    line[:, 2 * span :] = jnp.concatenate([high, share - high], axis=1).astype(BF)


def finish_kernel(own, up, down, out):
    order = out.shape[0] * CHIPS * CORES
    for i in range(own.shape[0]):
        acc = own[i] + up[i].astype(F32) + down[i].astype(F32)
        out[:, i, :] = acc * (1.0 / order)


def line_rows(q, k, sibling):
    core = q & 1
    chip = ((q >> 1) - k) & (CHIPS - 1)
    return chip * CORES + (core ^ sibling)


def forward_rows(q, k, sibling):
    core = q & 1
    chip = ((q >> 1) + k) & (CHIPS - 1)
    return chip * CORES + (core ^ sibling)


def put_line(q, k, sibling, piece, whole, target, share):
    few = piece.shape[1] // 17 // 2
    span = piece.shape[1] // 17 * 8
    place = line_rows(q, k, sibling)
    row = pl.multiple_of(place * span, span)
    whole[:, pl.ds(row, span), :] = piece[:, :span]
    target[:, pl.ds(row, span), :] = piece[:, span : 2 * span]
    parts = piece[:, 2 * span :].astype(F32)
    share[:, pl.ds(pl.multiple_of(place * few, few), few), :] = parts[:, :few] + parts[:, few:]


def place_plane(p, pieces, swap, whole, start, stop):
    span = pieces[0].shape[2]
    if len(pieces) == SIDE:
        parts = [(piece, d, 0) for d, piece in enumerate(pieces)]
    else:
        first, near, even, odd, far = pieces
        parts = [(first, 0, 0), (near, 1, 0), (even, 2, 0), (odd, 2, 1), (far, 3, 0)]
    for piece, d, low in parts:
        lo, hi = max(low, start), min(low + piece.shape[1], stop)
        if lo >= hi:
            continue
        for e in range(SIDE):
            dx, dy = (e, d) if swap else (d, e)
            x = ((p >> 2) - dx) & (SIDE - 1)
            y = ((p & 3) - dy) & (SIDE - 1)
            row = pl.multiple_of((x * SIDE + y) * span, span)
            whole[lo - start : hi - start, pl.ds(row, span), :] = piece[e, lo - low : hi - low]


def spread(q, i, source, keep, send, share=None):
    span = source.shape[0] // (CHIPS * CORES)
    for k in range(CHIPS):
        for sibling, out, kind in ((0, keep, F32), (1, send, BF)):
            place = forward_rows(q, k, sibling)
            row = pl.multiple_of(place * span, span)
            out[k, i, :span] = source[pl.ds(row, span), :].astype(kind)
            if share is not None:
                few = share.shape[0] // (CHIPS * CORES)
                part = share[pl.ds(pl.multiple_of(place * few, few), few), :]
                high = part if kind == F32 else part.astype(BF).astype(F32)
                out[k, i, span:] = jnp.concatenate([high, part - high], axis=0).astype(kind)


PIECES = SIDE + 1


def sample_kernel(tiles, columns):
    def kernel(p_ref, q_ref, ranks, left_hbm, right_hbm, tright, *refs):
        right_pieces, refs = refs[:SIDE], refs[SIDE:]
        left_pieces, refs = refs[:PIECES], refs[PIECES:]
        coupling, keep, send, lefts, pivot, probe, flip, ps, share, result, left, right, done = refs
        copies = [
            pltpu.make_async_copy(right_hbm, right, done.at[0]),
            pltpu.make_async_copy(left_hbm, left, done.at[1]),
        ]
        for copy in copies:
            copy.start()
        p, q = p_ref[0], q_ref[0]
        place_plane(p, left_pieces, True, lefts, 0, columns)
        place_plane(p, left_pieces, True, probe, columns, columns + 1)
        for j in range(columns):
            ps[j] = dims(lefts[j].T, probe[0], 1, 0)
        place_plane(p, right_pieces, False, pivot, 0, columns)
        for j in range(columns):
            flip[j] = pivot[j].T
        span = tright.shape[1]
        sketch = probe[0, pl.ds(pl.multiple_of(q * span, span), span), :]
        for copy in copies:
            copy.wait()

        def tile(i, carry):
            weights = []
            for j in range(columns):
                coup = dims(flip[j], right[i, j], 1, 0).T
                row = lax.broadcasted_iota(jnp.int32, coup.shape, 0)
                coup = jnp.where(row < ranks[i, j], coup, 0.0)
                coupling[i, j] = coup
                weights.append((-fine(coup, ps[j], 1, 0)).astype(BF))
            u = jnp.concatenate([left[i, j] for j in range(columns)], axis=1)
            share[...] = dims(tright[i], sketch, 0, 0)
            result[...] = dims(u, jnp.concatenate(weights, axis=0), 1, 0)
            spread(q, i, result, keep, send, share)
            return carry

        lax.fori_loop(0, tiles, tile, 0)

    return kernel


def eliminate(m, width):
    lane = lax.broadcasted_iota(jnp.int32, (8, width), 1)
    sub = lax.broadcasted_iota(jnp.int32, (8, width), 0)
    within = lane & (NB - 1)
    base = lane - within
    for k in range(0, NB, 2):
        b, r = k // 8, k % 8
        at0, at1 = within == k, within == k + 1
        g0 = [jnp.take_along_axis(m[n], base + k, axis=1) if n >= b else None for n in range(len(m))]
        g1 = [jnp.take_along_axis(m[n], base + (k + 1), axis=1) if n >= b else None for n in range(len(m))]
        row0, row1 = m[b][r : r + 1], m[b][r + 1 : r + 2]
        i0 = 1.0 / g0[b][r : r + 1]
        up, low = g1[b][r : r + 1], g0[b][r + 1 : r + 2]
        ratio = up * i0
        i1 = 1.0 / (g1[b][r + 1 : r + 2] - low * ratio)
        at0r, at1r = at0[:1], at1[:1]
        s0 = jnp.where(at0r, i0, row0 * i0)
        next_row = jnp.where(at0r, 0.0, row1) - low * s0
        s1 = jnp.where(at1r, i1, next_row * i1)
        s0 = jnp.where(at1r, 0.0, s0)
        for n in range(b, len(m)):
            new = jnp.where(at0 | at1, 0.0, m[n]) - g0[n] * s0 - (g1[n] - g0[n] * ratio) * s1
            if n == b:
                new = jnp.where(sub > r + 1, new, jnp.where(sub == r + 1, next_row, m[n]))
            m[n] = new
    return m


def factor_inverse(gram):
    tiles, rank, _ = gram.shape
    width = tiles * NB
    lane = lax.broadcasted_iota(jnp.int32, (NB, width), 1)
    row = lax.broadcasted_iota(jnp.int32, (NB, width), 0)
    within = lane & (NB - 1)
    square_row = lax.broadcasted_iota(jnp.int32, (width, width), 0)
    square_lane = lax.broadcasted_iota(jnp.int32, (width, width), 1)
    same = (square_row & -NB) == (square_lane & -NB)
    full_lane = lax.broadcasted_iota(jnp.int32, (rank, rank), 1)
    for start in range(0, rank, NB):
        stop = start + NB
        block = slice(start, stop)
        packed = jnp.concatenate([gram[i, block, block] for i in range(tiles)], axis=1)
        m = eliminate([packed[n : n + 8] for n in range(0, NB, 8)], width)
        m = jnp.concatenate(m, axis=0)
        pivots = jnp.take_along_axis(m, lane - within + row, axis=1)
        unit = jnp.where(within == row, 1.0, jnp.where(within < row, m, 0.0)) / jnp.sqrt(pivots)
        diagonal = jnp.where(same, jnp.concatenate([unit] * tiles, axis=0), 0.0)
        lines = fine(diagonal, jnp.concatenate([gram[i, block, :] for i in range(tiles)], axis=0), 1, 0)
        for i in range(tiles):
            line = lines[i * NB : (i + 1) * NB]
            own = pltpu.roll(unit, (start - i * NB) % width, 1) if (start - i * NB) % width else unit
            inside = (lane >= start) & (lane < stop)
            line = jnp.where(inside, own, line)
            gram[i, block, :] = jnp.where(lane < stop, line, 0.0)
            if stop < rank:
                update = fine(line, line, 0, 0)[stop:]
                rest = gram[i, stop:, :]
                zero = (full_lane[stop:] >= start) & (full_lane[stop:] < stop)
                gram[i, stop:, :] = jnp.where(zero, 0.0, rest) - update


def project_kernel(tiles, columns):
    def kernel(q_ref, left_hbm, coupling, tright, pivot, wide, *refs):
        line_pieces, refs = refs[:CHIPS], refs[CHIPS:]
        side_pieces, refs = refs[: len(SIDE_ORDER)], refs[len(SIDE_ORDER) :]
        exact, gram, keep, send, whole, target, share, flipped, result, left, done = refs
        copy = pltpu.make_async_copy(left_hbm, left, done)
        copy.start()
        q = q_ref[0]
        order = whole.shape[1]
        own = pl.ds(pl.multiple_of(q * wide.shape[1], wide.shape[1]), wide.shape[1])
        for k, piece in enumerate(line_pieces):
            put_line(q, k, 0, piece[...], whole, target, share)
        for piece, ks in zip(side_pieces, SIDE_ORDER):
            for n, k in enumerate(ks):
                put_line(q, k, 1, piece[n], whole, target, share)

        def square(i, carry):
            both = jnp.concatenate(halves(share[i]), axis=0)
            t = jnp.concatenate([target[i], target[i]], axis=1)
            term = dims(t, both, 1, 0)
            result[...] = term
            exact[i] = wide[i] + result[own, :]
            whole[i] = (whole[i].astype(F32) + term).astype(BF)
            flipped[i] = whole[i].T
            gram[i] = dims(flipped[i], whole[i], 1, 0) * (1.0 / order)
            return carry

        lax.fori_loop(0, tiles, square, 0)
        copy.wait()
        factor_inverse(gram)

        def tile(i, carry):
            inverse = gram[i]
            both = jnp.concatenate([left[i, j] for j in range(columns)], axis=1)
            seen = dims(flipped[i], both, 1, 0)
            span = inverse.shape[1]
            mixed = [
                fine(seen[:, j * span : (j + 1) * span], coupling[i, j], 1, 0) for j in range(columns)
            ]
            mixed.append(dims(flipped[i], target[i], 1, 0))
            solved = fine(inverse, jnp.concatenate(mixed, axis=1), 1, 0).astype(BF)
            u = jnp.concatenate([pivot[j] for j in range(columns)], axis=1)
            result[...] = -dims(u, solved[:, : columns * span], 1, 1)
            spread(q, i, result, keep, send)
            keep[0, i] = keep[0, i] + dims(tright[i], solved[:, columns * span :], 1, 1)
            return carry

        lax.fori_loop(0, tiles, tile, 0)

    return kernel


def vmem(n):
    return [pl.BlockSpec(memory_space=pltpu.VMEM)] * n


def basis_kernel(exact, inverse, out):
    for i in range(exact.shape[0]):
        out[:, i, :] = fine(exact[i], inverse[i], 1, 1)


def anywhere(n):
    return [pl.BlockSpec(memory_space=pl.ANY)] * n


def smem(n):
    return [pl.BlockSpec(memory_space=pltpu.SMEM)] * n


def per_device(
    left_factor, right_factor, pivot_left, pivot_right, target_left, target_right, probe, ranks
):
    tiles, columns, order, rank = left_factor.shape
    span = target_left.shape[0]
    n_col = CHIPS * CORES
    p = jnp.full((1,), lax.axis_index("prow"), jnp.int32)
    q = jnp.full((1,), lax.axis_index("pcol"), jnp.int32)
    right_first = first_stage(pivot_right, along_y)
    left_first = first_stage(jnp.concatenate([pivot_left, probe[None]]), along_x)
    right_plane = second_stage(right_first, along_x, "rights")
    left_plane = second_stage(left_first, along_y, "lefts")
    left_own = jnp.transpose(target_left, (1, 0, 2))
    right_own = jnp.transpose(target_right, (1, 0, 2))

    few = 2 * rank // n_col
    tall = (CHIPS, tiles, span + few, rank)
    coupling, keep, send, pivot = pl.pallas_call(
        sample_kernel(tiles, columns),
        out_shape=[
            jax.ShapeDtypeStruct((tiles, columns, rank, rank), F32),
            jax.ShapeDtypeStruct(tall, F32),
            jax.ShapeDtypeStruct(tall, BF),
            jax.ShapeDtypeStruct((columns, order, rank), BF),
        ],
        in_specs=smem(3) + anywhere(2) + vmem(1 + SIDE + PIECES),
        scratch_shapes=[
            pltpu.VMEM((columns, order, rank), BF),
            pltpu.VMEM((1, order, rank), BF),
            pltpu.VMEM((columns, rank, order), BF),
            pltpu.VMEM((columns, rank, rank), F32),
            pltpu.VMEM((rank, rank), F32),
            pltpu.VMEM((order, rank), F32),
            pltpu.VMEM(left_factor.shape, BF),
            pltpu.VMEM(left_factor.shape, BF),
            pltpu.SemaphoreType.DMA((2,)),
        ],
        name="sample",
    )(p, q, ranks, left_factor, right_factor, right_own, *right_plane, *left_plane)

    wide, line = pl.pallas_call(
        samples_kernel,
        out_shape=[
            jax.ShapeDtypeStruct((tiles, span, rank), F32),
            jax.ShapeDtypeStruct((tiles, 2 * span + few, rank), BF),
        ],
        name="samples_sum",
    )(*scatter_line(keep, send, F32, few // 2), left_own)

    share = (CHIPS, tiles, span, rank)
    exact, inverse, keep, send = pl.pallas_call(
        project_kernel(tiles, columns),
        out_shape=[
            jax.ShapeDtypeStruct((tiles, span, rank), F32),
            jax.ShapeDtypeStruct((tiles, rank, rank), F32),
            jax.ShapeDtypeStruct(share, F32),
            jax.ShapeDtypeStruct(share, BF),
        ],
        in_specs=smem(1) + anywhere(1) + vmem(4 + CHIPS + len(SIDE_ORDER)),
        scratch_shapes=[
            pltpu.VMEM((tiles, order, rank), BF),
            pltpu.VMEM((tiles, order, rank), BF),
            pltpu.VMEM((tiles, rank, rank), F32),
            pltpu.VMEM((tiles, rank, order), BF),
            pltpu.VMEM((order, rank), F32),
            pltpu.VMEM(left_factor.shape, BF),
            pltpu.SemaphoreType.DMA,
        ],
        name="project",
    )(q, left_factor, coupling, right_own, pivot, wide, *gather_line(line))
    basis = pl.pallas_call(
        basis_kernel, out_shape=jax.ShapeDtypeStruct((span, tiles, rank), F32), name="basis"
    )(exact, inverse)
    coefficient = pl.pallas_call(
        finish_kernel,
        out_shape=jax.ShapeDtypeStruct((span, tiles, rank), F32),
        name="finish",
    )(*scatter_line(keep, send, BF, 0))
    return (basis, coefficient)


def solution(mesh):
    in_specs = (
        P("prow", "pcol", None, None),
        P("prow", "pcol", None, None),
        P("pcol", "prow", None),
        P("pcol", "prow", None),
        P("pcol", "prow", None),
        P("pcol", "prow", None),
        P("prow", None),
        P("prow", "pcol"),
    )
    out_specs = (P("pcol", "prow", None), P("pcol", "prow", None))

    return jax.shard_map(per_device, mesh=mesh, in_specs=in_specs, out_specs=out_specs, check_vma=False)
```

```python
import jax
import jax.numpy as jnp
from jax import lax
from jax.experimental import pallas as pl
from jax.experimental.pallas import tpu as pltpu
from jax.sharding import PartitionSpec as P


F32 = jnp.float32
BF = jnp.bfloat16
SIDE = 4
CHIPS = 8
CORES = 2
NB = 32


def dims(a, b, ca, cb, precision=None):
    return lax.dot_general(
        a, b, (((ca,), (cb,)), ((), ())), precision=precision, preferred_element_type=F32
    )


def halves(v):
    high = v.astype(BF)
    return high, (v - high.astype(F32)).astype(BF)


def fine(a, b, ca, cb):
    ah, al = halves(a)
    bh, bl = halves(b)
    return dims(ah, bh, ca, cb) + (dims(ah, bl, ca, cb) + dims(al, bh, ca, cb))


def to_sibling(v):
    return lax.ppermute(v, "pcol", [(i, i ^ 1) for i in range(CHIPS * CORES)])


def along_z(v, k):
    n = CHIPS * CORES
    return lax.ppermute(v, "pcol", [(i, (i + CORES * k) % n) for i in range(n)])


def along_y(v, d):
    return lax.ppermute(
        v, "prow", [(SIDE * x + y, SIDE * x + (y + d) % SIDE) for x in range(SIDE) for y in range(SIDE)]
    )


def along_x(v, d):
    return lax.ppermute(
        v, "prow", [(SIDE * x + y, SIDE * ((x + d) % SIDE) + y) for x in range(SIDE) for y in range(SIDE)]
    )


def first_stage(v, along):
    parts = [along(v, d) for d in (1, 2, -1)]
    return jnp.stack([v, *parts])


def second_stage(stacked, along, tag):
    far = along(stacked, -1)
    near = along(stacked, 1)
    if tag == "rights":
        return [stacked, near, along(stacked, 2), far]
    even = along(stacked[:, :1], 2)
    return [stacked, near, even, along(far[:, 1:], -1), far]


def gather_line(v):
    up = [v]
    down = [v]
    for step in range(CHIPS // 2):
        up.append(along_z(up[-1], 1))
        if step < CHIPS // 2 - 1:
            down.append(along_z(down[-1], -1))
    first = to_sibling(stack(up[0], up[1], up[2], down[1]))
    second = to_sibling(stack(down[2], down[3], up[3]))
    return up + down[:0:-1] + [first, second, to_sibling(up[4][None])]


SIDE_ORDER = ((0, 1, 2, -1), (-2, -3, 3), (4,))


def scatter_line(keep, send, down_type, few):
    other = to_sibling(send)
    half = CHIPS // 2

    def share(k):
        return keep[k] + other[k].astype(F32)

    up, down, own = share(half).astype(BF), share(half + 1).astype(down_type), share(0)
    for k in range(half - 1, 0, -1):
        up = along_z(up, 1)
        split = few and k == 1
        up = onward(up, keep, other, k, few) if split else (up.astype(F32) + share(k)).astype(BF)
        down = along_z(down, -1)
        if k > 1:
            down = (down.astype(F32) + share(CHIPS - k + 1)).astype(down_type)
    return own, along_z(up, 1), down


def narrow(out, value, few):
    if not few:
        out[...] = value.astype(BF)
        return
    span = value.shape[1] - 2 * few
    out[:, :span] = value[:, :span].astype(BF)
    whole = value[:, span : span + few] + value[:, span + few :]
    high = whole.astype(BF).astype(F32)
    out[:, span:] = jnp.concatenate([high, whole - high], axis=1).astype(BF)


def block(shape, k):
    return pl.BlockSpec((1, *shape), lambda _: (k, *[0] * len(shape)))


def onward(got, keep, other, k, few):
    shape = keep.shape[1:]
    plain = pl.BlockSpec(shape, lambda _: (0,) * len(shape))

    def kernel(g, k0, o0, out):
        narrow(out, g[...].astype(F32) + k0[0] + o0[0].astype(F32), few)

    return pl.pallas_call(
        kernel,
        grid=(1,),
        in_specs=[plain, block(shape, k), block(shape, k)],
        out_specs=plain,
        out_shape=jax.ShapeDtypeStruct(shape, BF),
        name="onward",
    )(got, keep, other)


def stack_kernel(*refs):
    out = refs[-1]
    for n, ref in enumerate(refs[:-1]):
        out[n] = ref[...]


def stack(*parts):
    return pl.pallas_call(
        stack_kernel,
        out_shape=jax.ShapeDtypeStruct((len(parts), *parts[0].shape), parts[0].dtype),
        name="stack",
    )(*parts)


def samples_kernel(own, up, down, target, wide, line):
    acc = own[...] + up[...].astype(F32) + down[...].astype(F32)
    span = target.shape[1]
    few = (acc.shape[1] - span) // 2
    wide[...] = acc[:, :span]
    line[:, :span] = acc[:, :span].astype(BF)
    line[:, span : 2 * span] = target[...]
    share = acc[:, span : span + few] + acc[:, span + few :]
    high = share.astype(BF).astype(F32)
    line[:, 2 * span :] = jnp.concatenate([high, share - high], axis=1).astype(BF)


def finish_kernel(own, up, down, out):
    order = out.shape[0] * CHIPS * CORES
    for i in range(own.shape[0]):
        acc = own[i] + up[i].astype(F32) + down[i].astype(F32)
        out[:, i, :] = acc * (1.0 / order)


def line_rows(q, k, sibling):
    core = q & 1
    chip = ((q >> 1) - k) & (CHIPS - 1)
    return chip * CORES + (core ^ sibling)


def forward_rows(q, k, sibling):
    core = q & 1
    chip = ((q >> 1) + k) & (CHIPS - 1)
    return chip * CORES + (core ^ sibling)


def put_line(q, k, sibling, piece, whole, target, share):
    few = piece.shape[1] // 17 // 2
    span = piece.shape[1] // 17 * 8
    place = line_rows(q, k, sibling)
    row = pl.multiple_of(place * span, span)
    whole[:, pl.ds(row, span), :] = piece[:, :span]
    target[:, pl.ds(row, span), :] = piece[:, span : 2 * span]
    parts = piece[:, 2 * span :].astype(F32)
    share[:, pl.ds(pl.multiple_of(place * few, few), few), :] = parts[:, :few] + parts[:, few:]


def place_plane(p, pieces, swap, whole, start, stop):
    span = pieces[0].shape[2]
    if len(pieces) == SIDE:
        parts = [(piece, d, 0) for d, piece in enumerate(pieces)]
    else:
        first, near, even, odd, far = pieces
        parts = [(first, 0, 0), (near, 1, 0), (even, 2, 0), (odd, 2, 1), (far, 3, 0)]
    for piece, d, low in parts:
        lo, hi = max(low, start), min(low + piece.shape[1], stop)
        if lo >= hi:
            continue
        for e in range(SIDE):
            dx, dy = (e, d) if swap else (d, e)
            x = ((p >> 2) - dx) & (SIDE - 1)
            y = ((p & 3) - dy) & (SIDE - 1)
            row = pl.multiple_of((x * SIDE + y) * span, span)
            whole[lo - start : hi - start, pl.ds(row, span), :] = piece[e, lo - low : hi - low]


def in_turn(q, sources):
    span = sources[0].shape[0] // (CHIPS * CORES)
    columns = []
    for source in sources:
        rows = []
        for sibling in range(CORES):
            for k in range(CHIPS):
                row = pl.multiple_of(forward_rows(q, k, sibling) * span, span)
                rows.append(source[pl.ds(row, span), :])
        columns.append(jnp.concatenate(rows, axis=0))
    return jnp.concatenate(columns, axis=1)


def spread(q, i, value, keep, send, share=None):
    span = value.shape[0] // (CHIPS * CORES)
    for sibling, out, kind in ((0, keep, F32), (1, send, BF)):
        for k in range(CHIPS):
            at = (sibling * CHIPS + k) * span
            out[k, i, :span] = value[at : at + span].astype(kind)
            if share is not None:
                few = share.shape[0] // (CHIPS * CORES)
                place = forward_rows(q, k, sibling)
                part = share[pl.ds(pl.multiple_of(place * few, few), few), :]
                high = part if kind == F32 else part.astype(BF).astype(F32)
                out[k, i, span:] = jnp.concatenate([high, part - high], axis=0).astype(kind)


PIECES = SIDE + 1


def sample_kernel(tiles, columns):
    def kernel(p_ref, q_ref, ranks, left_hbm, right_hbm, tright, *refs):
        right_pieces, refs = refs[:SIDE], refs[SIDE:]
        left_pieces, refs = refs[:PIECES], refs[PIECES:]
        coupling, keep, send, lefts, pivot, probe, flip, ps, share, left, right, done = refs
        copies = [
            pltpu.make_async_copy(right_hbm, right, done.at[0]),
            pltpu.make_async_copy(left_hbm, left, done.at[1]),
        ]
        for copy in copies:
            copy.start()
        p, q = p_ref[0], q_ref[0]
        place_plane(p, left_pieces, True, lefts, 0, columns)
        place_plane(p, left_pieces, True, probe, columns, columns + 1)
        for j in range(columns):
            ps[j] = dims(lefts[j].T, probe[0], 1, 0)
        place_plane(p, right_pieces, False, pivot, 0, columns)
        for j in range(columns):
            flip[j] = pivot[j].T
        span = tright.shape[1]
        sketch = probe[0, pl.ds(pl.multiple_of(q * span, span), span), :]
        for copy in copies:
            copy.wait()

        def tile(i, carry):
            weights = []
            for j in range(columns):
                coup = dims(flip[j], right[i, j], 1, 0).T
                row = lax.broadcasted_iota(jnp.int32, coup.shape, 0)
                coup = jnp.where(row < ranks[i, j], coup, 0.0)
                coupling[i, j] = coup
                weights.append((-fine(coup, ps[j], 1, 0)).astype(BF))
            u = in_turn(q, [left.at[i, j] for j in range(columns)])
            share[...] = dims(tright[i], sketch, 0, 0)
            spread(q, i, dims(u, jnp.concatenate(weights, axis=0), 1, 0), keep, send, share)
            return carry

        lax.fori_loop(0, tiles, tile, 0)

    return kernel


def eliminate(m, width):
    lane = lax.broadcasted_iota(jnp.int32, (8, width), 1)
    sub = lax.broadcasted_iota(jnp.int32, (8, width), 0)
    within = lane & (NB - 1)
    base = lane - within
    for k in range(0, NB, 2):
        b, r = k // 8, k % 8
        at0, at1 = within == k, within == k + 1
        g0 = [jnp.take_along_axis(m[n], base + k, axis=1) if n >= b else None for n in range(len(m))]
        g1 = [jnp.take_along_axis(m[n], base + (k + 1), axis=1) if n >= b else None for n in range(len(m))]
        row0, row1 = m[b][r : r + 1], m[b][r + 1 : r + 2]
        i0 = 1.0 / g0[b][r : r + 1]
        up, low = g1[b][r : r + 1], g0[b][r + 1 : r + 2]
        ratio = up * i0
        i1 = 1.0 / (g1[b][r + 1 : r + 2] - low * ratio)
        at0r, at1r = at0[:1], at1[:1]
        s0 = jnp.where(at0r, i0, row0 * i0)
        next_row = jnp.where(at0r, 0.0, row1) - low * s0
        s1 = jnp.where(at1r, i1, next_row * i1)
        s0 = jnp.where(at1r, 0.0, s0)
        for n in range(b, len(m)):
            new = jnp.where(at0 | at1, 0.0, m[n]) - g0[n] * s0 - (g1[n] - g0[n] * ratio) * s1
            if n == b:
                new = jnp.where(sub > r + 1, new, jnp.where(sub == r + 1, next_row, m[n]))
            m[n] = new
    return m


def factor_inverse(gram):
    tiles, rank, _ = gram.shape
    width = tiles * NB
    lane = lax.broadcasted_iota(jnp.int32, (NB, width), 1)
    row = lax.broadcasted_iota(jnp.int32, (NB, width), 0)
    within = lane & (NB - 1)
    square_row = lax.broadcasted_iota(jnp.int32, (width, width), 0)
    square_lane = lax.broadcasted_iota(jnp.int32, (width, width), 1)
    same = (square_row & -NB) == (square_lane & -NB)

    def step(n, carry):
        start = pl.multiple_of(n * NB, NB)
        stop = start + NB
        block = pl.ds(start, NB)
        rows = [gram[i, block, :] for i in range(tiles)]
        packed = jnp.zeros((NB, width), F32)
        for i in range(tiles):
            moved = pltpu.roll(rows[i], (i * NB - start) & (width - 1), 1)
            packed = jnp.where(lane - within == i * NB, moved, packed)
        m = eliminate([packed[k : k + 8] for k in range(0, NB, 8)], width)
        m = jnp.concatenate(m, axis=0)
        pivots = jnp.take_along_axis(m, lane - within + row, axis=1)
        unit = jnp.where(within == row, 1.0, jnp.where(within < row, m, 0.0)) / jnp.sqrt(pivots)
        diagonal = jnp.where(same, jnp.concatenate([unit] * tiles, axis=0), 0.0)
        lines = fine(diagonal, jnp.concatenate(rows, axis=0), 1, 0)
        inside = (lane >= start) & (lane < stop)
        for i in range(tiles):
            own = pltpu.roll(unit, (start - i * NB) & (width - 1), 1)
            line = jnp.where(inside, own, lines[i * NB : (i + 1) * NB])
            gram[i, block, :] = jnp.where(lane < stop, line, 0.0)
            rest = gram[i]
            kept = jnp.where((square_lane >= start) & (square_lane < stop), 0.0, rest)
            gram[i] = jnp.where(square_row >= stop, kept - fine(line, line, 0, 0), rest)
        return carry

    lax.fori_loop(0, rank // NB, step, 0)


def project_kernel(tiles, columns):
    def kernel(q_ref, left_hbm, coupling, tright, pivot, wide, *refs):
        line_pieces, refs = refs[:CHIPS], refs[CHIPS:]
        side_pieces, refs = refs[: len(SIDE_ORDER)], refs[len(SIDE_ORDER) :]
        exact, gram, keep, send, whole, target, share, flipped, left, done = refs
        copy = pltpu.make_async_copy(left_hbm, left, done)
        copy.start()
        q = q_ref[0]
        order = whole.shape[1]
        own = pl.ds(pl.multiple_of(q * wide.shape[1], wide.shape[1]), wide.shape[1])
        for k, piece in enumerate(line_pieces):
            put_line(q, k, 0, piece[...], whole, target, share)
        for piece, ks in zip(side_pieces, SIDE_ORDER):
            for n, k in enumerate(ks):
                put_line(q, k, 1, piece[n], whole, target, share)

        def square(i, carry):
            both = jnp.concatenate(halves(share[i]), axis=0)
            t = jnp.concatenate([target[i], target[i]], axis=1)
            t_own = jnp.concatenate([target[i, own, :], target[i, own, :]], axis=1)
            exact[i] = wide[i] + dims(t_own, both, 1, 0)
            whole[i] = (whole[i].astype(F32) + dims(t, both, 1, 0)).astype(BF)
            flipped[i] = whole[i].T
            gram[i] = dims(flipped[i], whole[i], 1, 0) * (1.0 / order)
            return carry

        lax.fori_loop(0, tiles, square, 0, unroll=2)
        copy.wait()
        factor_inverse(gram)

        def tile(i, carry):
            inverse = gram[i]
            both = jnp.concatenate([left[i, j] for j in range(columns)], axis=1)
            seen = dims(flipped[i], both, 1, 0)
            span = inverse.shape[1]
            mixed = [
                fine(seen[:, j * span : (j + 1) * span], coupling[i, j], 1, 0) for j in range(columns)
            ]
            mixed.append(dims(flipped[i], target[i], 1, 0))
            solved = fine(inverse, jnp.concatenate(mixed, axis=1), 1, 0).astype(BF)
            u = in_turn(q, [pivot.at[j] for j in range(columns)])
            spread(q, i, dims(u, -solved[:, : columns * span], 1, 1), keep, send)
            keep[0, i] = keep[0, i] + dims(tright[i], solved[:, columns * span :], 1, 1)
            return carry

        lax.fori_loop(0, tiles, tile, 0, unroll=2)

    return kernel


def vmem(n):
    return [pl.BlockSpec(memory_space=pltpu.VMEM)] * n


def basis_kernel(exact, inverse, out):
    for i in range(exact.shape[0]):
        out[:, i, :] = fine(exact[i], inverse[i], 1, 1)


def anywhere(n):
    return [pl.BlockSpec(memory_space=pl.ANY)] * n


def smem(n):
    return [pl.BlockSpec(memory_space=pltpu.SMEM)] * n


def per_device(
    left_factor, right_factor, pivot_left, pivot_right, target_left, target_right, probe, ranks
):
    tiles, columns, order, rank = left_factor.shape
    span = target_left.shape[0]
    n_col = CHIPS * CORES
    p = jnp.full((1,), lax.axis_index("prow"), jnp.int32)
    q = jnp.full((1,), lax.axis_index("pcol"), jnp.int32)
    right_first = first_stage(pivot_right, along_y)
    left_first = first_stage(jnp.concatenate([pivot_left, probe[None]]), along_x)
    right_plane = second_stage(right_first, along_x, "rights")
    left_plane = second_stage(left_first, along_y, "lefts")
    left_own = jnp.transpose(target_left, (1, 0, 2))
    right_own = jnp.transpose(target_right, (1, 0, 2))

    few = 2 * rank // n_col
    tall = (CHIPS, tiles, span + few, rank)
    coupling, keep, send, pivot = pl.pallas_call(
        sample_kernel(tiles, columns),
        out_shape=[
            jax.ShapeDtypeStruct((tiles, columns, rank, rank), F32),
            jax.ShapeDtypeStruct(tall, F32),
            jax.ShapeDtypeStruct(tall, BF),
            jax.ShapeDtypeStruct((columns, order, rank), BF),
        ],
        in_specs=smem(3) + anywhere(2) + vmem(1 + SIDE + PIECES),
        scratch_shapes=[
            pltpu.VMEM((columns, order, rank), BF),
            pltpu.VMEM((1, order, rank), BF),
            pltpu.VMEM((columns, rank, order), BF),
            pltpu.VMEM((columns, rank, rank), F32),
            pltpu.VMEM((rank, rank), F32),
            pltpu.VMEM(left_factor.shape, BF),
            pltpu.VMEM(left_factor.shape, BF),
            pltpu.SemaphoreType.DMA((2,)),
        ],
        name="sample",
    )(p, q, ranks, left_factor, right_factor, right_own, *right_plane, *left_plane)

    wide, line = pl.pallas_call(
        samples_kernel,
        out_shape=[
            jax.ShapeDtypeStruct((tiles, span, rank), F32),
            jax.ShapeDtypeStruct((tiles, 2 * span + few, rank), BF),
        ],
        name="samples_sum",
    )(*scatter_line(keep, send, F32, few // 2), left_own)

    share = (CHIPS, tiles, span, rank)
    exact, inverse, keep, send = pl.pallas_call(
        project_kernel(tiles, columns),
        out_shape=[
            jax.ShapeDtypeStruct((tiles, span, rank), F32),
            jax.ShapeDtypeStruct((tiles, rank, rank), F32),
            jax.ShapeDtypeStruct(share, F32),
            jax.ShapeDtypeStruct(share, BF),
        ],
        in_specs=smem(1) + anywhere(1) + vmem(4 + CHIPS + len(SIDE_ORDER)),
        scratch_shapes=[
            pltpu.VMEM((tiles, order, rank), BF),
            pltpu.VMEM((tiles, order, rank), BF),
            pltpu.VMEM((tiles, rank, rank), F32),
            pltpu.VMEM((tiles, rank, order), BF),
            pltpu.VMEM(left_factor.shape, BF),
            pltpu.SemaphoreType.DMA,
        ],
        name="project",
    )(q, left_factor, coupling, right_own, pivot, wide, *gather_line(line))
    basis = pl.pallas_call(
        basis_kernel, out_shape=jax.ShapeDtypeStruct((span, tiles, rank), F32), name="basis"
    )(exact, inverse)
    coefficient = pl.pallas_call(
        finish_kernel,
        out_shape=jax.ShapeDtypeStruct((span, tiles, rank), F32),
        name="finish",
    )(*scatter_line(keep, send, BF, 0))
    return (basis, coefficient)


def solution(mesh):
    in_specs = (
        P("prow", "pcol", None, None),
        P("prow", "pcol", None, None),
        P("pcol", "prow", None),
        P("pcol", "prow", None),
        P("pcol", "prow", None),
        P("pcol", "prow", None),
        P("prow", None),
        P("prow", "pcol"),
    )
    out_specs = (P("pcol", "prow", None), P("pcol", "prow", None))

    return jax.shard_map(per_device, mesh=mesh, in_specs=in_specs, out_specs=out_specs, check_vma=False)
```

```python
import jax
import jax.numpy as jnp
from jax import lax
from jax.experimental import pallas as pl
from jax.experimental.pallas import tpu as pltpu
from jax.sharding import PartitionSpec as P


F32 = jnp.float32
BF = jnp.bfloat16
SIDE = 4
CHIPS = 8
CORES = 2
NB = 32


def dims(a, b, ca, cb, precision=None):
    return lax.dot_general(
        a, b, (((ca,), (cb,)), ((), ())), precision=precision, preferred_element_type=F32
    )


def halves(v):
    high = v.astype(BF)
    return high, (v - high.astype(F32)).astype(BF)


def fine(a, b, ca, cb):
    ah, al = halves(a)
    bh, bl = halves(b)
    return dims(ah, bh, ca, cb) + (dims(ah, bl, ca, cb) + dims(al, bh, ca, cb))


def to_sibling(v):
    return lax.ppermute(v, "pcol", [(i, i ^ 1) for i in range(CHIPS * CORES)])


def along_z(v, k):
    n = CHIPS * CORES
    return lax.ppermute(v, "pcol", [(i, (i + CORES * k) % n) for i in range(n)])


def along_y(v, d):
    return lax.ppermute(
        v, "prow", [(SIDE * x + y, SIDE * x + (y + d) % SIDE) for x in range(SIDE) for y in range(SIDE)]
    )


def along_x(v, d):
    return lax.ppermute(
        v, "prow", [(SIDE * x + y, SIDE * ((x + d) % SIDE) + y) for x in range(SIDE) for y in range(SIDE)]
    )


def first_stage(v, along):
    parts = [along(v, d) for d in (1, 2, -1)]
    return jnp.stack([v, *parts])


def second_stage(stacked, along, tag):
    far = along(stacked, -1)
    near = along(stacked, 1)
    if tag == "rights":
        return [stacked, near, along(stacked, 2), far]
    even = along(stacked[:, :1], 2)
    return [stacked, near, even, along(far[:, 1:], -1), far]


def gather_line(v):
    up = [v]
    down = [v]
    for step in range(CHIPS // 2):
        up.append(along_z(up[-1], 1))
        if step < CHIPS // 2 - 1:
            down.append(along_z(down[-1], -1))
    first = to_sibling(stack(up[0], up[1], up[2], down[1]))
    second = to_sibling(stack(down[2], down[3], up[3]))
    return up + down[:0:-1] + [first, second, to_sibling(up[4][None])]


SIDE_ORDER = ((0, 1, 2, -1), (-2, -3, 3), (4,))


def scatter_line(keep, send, down_type, few):
    other = to_sibling(send)
    half = CHIPS // 2

    def share(k):
        return keep[k] + other[k].astype(F32)

    if few:
        up, down, own = begin(keep, other, few, down_type)
    else:
        up, down, own = share(half).astype(BF), share(half + 1).astype(down_type), share(0)
    for k in range(half - 1, 0, -1):
        up = along_z(up, 1)
        up = onward(up, keep, other, k, few) if few else (up.astype(F32) + share(k)).astype(BF)
        down = along_z(down, -1)
        if k > 1:
            down = (down.astype(F32) + share(CHIPS - k + 1)).astype(down_type)
    return own, along_z(up, 1), down


def narrow(out, value, few):
    if not few:
        out[...] = value.astype(BF)
        return
    span = value.shape[1] - 2 * few
    out[:, :span] = value[:, :span].astype(BF)
    whole = value[:, span : span + few] + value[:, span + few :]
    high = whole.astype(BF).astype(F32)
    out[:, span:] = jnp.concatenate([high, whole - high], axis=1).astype(BF)


def block(shape, k):
    return pl.BlockSpec((1, *shape), lambda _: (k, *[0] * len(shape)))


def begin(keep, other, few, down_type):
    shape = keep.shape[1:]
    half = CHIPS // 2

    def kernel(k0, k1, k2, o0, o1, o2, up, down, own):
        narrow(up, k0[0] + o0[0].astype(F32), few)
        down[...] = (k1[0] + o1[0].astype(F32)).astype(down_type)
        own[...] = k2[0] + o2[0].astype(F32)

    blocks = [block(shape, k) for k in (half, half + 1, 0)]
    return pl.pallas_call(
        kernel,
        grid=(1,),
        in_specs=blocks + blocks,
        out_specs=[pl.BlockSpec(shape, lambda _: (0,) * len(shape))] * 3,
        out_shape=[jax.ShapeDtypeStruct(shape, t) for t in (BF, down_type, F32)],
        name="begin",
    )(keep, keep, keep, other, other, other)


def onward(got, keep, other, k, few):
    shape = keep.shape[1:]
    plain = pl.BlockSpec(shape, lambda _: (0,) * len(shape))

    def kernel(g, k0, o0, out):
        narrow(out, g[...].astype(F32) + k0[0] + o0[0].astype(F32), few)

    return pl.pallas_call(
        kernel,
        grid=(1,),
        in_specs=[plain, block(shape, k), block(shape, k)],
        out_specs=plain,
        out_shape=jax.ShapeDtypeStruct(shape, BF),
        name="onward",
    )(got, keep, other)


def stack_kernel(*refs):
    out = refs[-1]
    for n, ref in enumerate(refs[:-1]):
        out[n] = ref[...]


def stack(*parts):
    return pl.pallas_call(
        stack_kernel,
        out_shape=jax.ShapeDtypeStruct((len(parts), *parts[0].shape), parts[0].dtype),
        name="stack",
    )(*parts)


def samples_kernel(own, up, down, target, wide, line):
    acc = own[...] + up[...].astype(F32) + down[...].astype(F32)
    span = target.shape[1]
    few = (acc.shape[1] - span) // 2
    wide[...] = acc[:, :span]
    line[:, :span] = acc[:, :span].astype(BF)
    line[:, span : 2 * span] = target[...]
    share = acc[:, span : span + few] + acc[:, span + few :]
    high = share.astype(BF).astype(F32)
    line[:, 2 * span :] = jnp.concatenate([high, share - high], axis=1).astype(BF)


def finish_kernel(own, up, down, out):
    order = out.shape[0] * CHIPS * CORES
    for i in range(own.shape[0]):
        acc = own[i] + up[i].astype(F32) + down[i].astype(F32)
        out[:, i, :] = acc * (1.0 / order)


def line_rows(q, k, sibling):
    core = q & 1
    chip = ((q >> 1) - k) & (CHIPS - 1)
    return chip * CORES + (core ^ sibling)


def forward_rows(q, k, sibling):
    core = q & 1
    chip = ((q >> 1) + k) & (CHIPS - 1)
    return chip * CORES + (core ^ sibling)


def put_line(q, k, sibling, piece, whole, target, share):
    few = piece.shape[1] // 17 // 2
    span = piece.shape[1] // 17 * 8
    place = line_rows(q, k, sibling)
    row = pl.multiple_of(place * span, span)
    whole[:, pl.ds(row, span), :] = piece[:, :span]
    target[:, pl.ds(row, span), :] = piece[:, span : 2 * span]
    parts = piece[:, 2 * span :].astype(F32)
    share[:, pl.ds(pl.multiple_of(place * few, few), few), :] = parts[:, :few] + parts[:, few:]


def place_plane(p, pieces, swap, whole, start, stop):
    span = pieces[0].shape[2]
    if len(pieces) == SIDE:
        parts = [(piece, d, 0) for d, piece in enumerate(pieces)]
    else:
        first, near, even, odd, far = pieces
        parts = [(first, 0, 0), (near, 1, 0), (even, 2, 0), (odd, 2, 1), (far, 3, 0)]
    for piece, d, low in parts:
        lo, hi = max(low, start), min(low + piece.shape[1], stop)
        if lo >= hi:
            continue
        for e in range(SIDE):
            dx, dy = (e, d) if swap else (d, e)
            x = ((p >> 2) - dx) & (SIDE - 1)
            y = ((p & 3) - dy) & (SIDE - 1)
            row = pl.multiple_of((x * SIDE + y) * span, span)
            whole[lo - start : hi - start, pl.ds(row, span), :] = piece[e, lo - low : hi - low]


def in_turn(q, sources):
    span = sources[0].shape[0] // (CHIPS * CORES)
    columns = []
    for source in sources:
        rows = []
        for sibling in range(CORES):
            for k in range(CHIPS):
                row = pl.multiple_of(forward_rows(q, k, sibling) * span, span)
                rows.append(source[pl.ds(row, span), :])
        columns.append(jnp.concatenate(rows, axis=0))
    return jnp.concatenate(columns, axis=1)


def spread(q, i, value, keep, send, share=None):
    span = value.shape[0] // (CHIPS * CORES)
    for sibling, out, kind in ((0, keep, F32), (1, send, BF)):
        for k in range(CHIPS):
            at = (sibling * CHIPS + k) * span
            out[k, i, :span] = value[at : at + span].astype(kind)
            if share is not None:
                few = share.shape[0] // (CHIPS * CORES)
                place = forward_rows(q, k, sibling)
                part = share[pl.ds(pl.multiple_of(place * few, few), few), :]
                high = part if kind == F32 else part.astype(BF).astype(F32)
                out[k, i, span:] = jnp.concatenate([high, part - high], axis=0).astype(kind)


PIECES = SIDE + 1


def sample_kernel(tiles, columns):
    def kernel(p_ref, q_ref, ranks, left_hbm, right_hbm, tright, *refs):
        right_pieces, refs = refs[:SIDE], refs[SIDE:]
        left_pieces, refs = refs[:PIECES], refs[PIECES:]
        coupling, keep, send, lefts, pivot, probe, flip, ps, share, left, right, done = refs
        copies = [
            pltpu.make_async_copy(right_hbm, right, done.at[0]),
            pltpu.make_async_copy(left_hbm, left, done.at[1]),
        ]
        for copy in copies:
            copy.start()
        p, q = p_ref[0], q_ref[0]
        place_plane(p, left_pieces, True, lefts, 0, columns)
        place_plane(p, left_pieces, True, probe, columns, columns + 1)
        for j in range(columns):
            ps[j] = dims(lefts[j].T, probe[0], 1, 0)
        place_plane(p, right_pieces, False, pivot, 0, columns)
        for j in range(columns):
            flip[j] = pivot[j].T
        span = tright.shape[1]
        sketch = probe[0, pl.ds(pl.multiple_of(q * span, span), span), :]
        for copy in copies:
            copy.wait()

        def tile(i, carry):
            weights = []
            for j in range(columns):
                coup = dims(flip[j], right[i, j], 1, 0).T
                row = lax.broadcasted_iota(jnp.int32, coup.shape, 0)
                coup = jnp.where(row < ranks[i, j], coup, 0.0)
                coupling[i, j] = coup
                weights.append((-fine(coup, ps[j], 1, 0)).astype(BF))
            u = in_turn(q, [left.at[i, j] for j in range(columns)])
            share[...] = dims(tright[i], sketch, 0, 0)
            spread(q, i, dims(u, jnp.concatenate(weights, axis=0), 1, 0), keep, send, share)
            return carry

        lax.fori_loop(0, tiles, tile, 0)

    return kernel


def eliminate(m, width):
    lane = lax.broadcasted_iota(jnp.int32, (8, width), 1)
    sub = lax.broadcasted_iota(jnp.int32, (8, width), 0)
    within = lane & (NB - 1)
    base = lane - within
    for k in range(0, NB, 2):
        b, r = k // 8, k % 8
        at0, at1 = within == k, within == k + 1
        g0 = [jnp.take_along_axis(m[n], base + k, axis=1) if n >= b else None for n in range(len(m))]
        g1 = [jnp.take_along_axis(m[n], base + (k + 1), axis=1) if n >= b else None for n in range(len(m))]
        row0, row1 = m[b][r : r + 1], m[b][r + 1 : r + 2]
        i0 = 1.0 / g0[b][r : r + 1]
        up, low = g1[b][r : r + 1], g0[b][r + 1 : r + 2]
        ratio = up * i0
        i1 = 1.0 / (g1[b][r + 1 : r + 2] - low * ratio)
        at0r, at1r = at0[:1], at1[:1]
        s0 = jnp.where(at0r, i0, row0 * i0)
        next_row = jnp.where(at0r, 0.0, row1) - low * s0
        s1 = jnp.where(at1r, i1, next_row * i1)
        s0 = jnp.where(at1r, 0.0, s0)
        for n in range(b, len(m)):
            new = jnp.where(at0 | at1, 0.0, m[n]) - g0[n] * s0 - (g1[n] - g0[n] * ratio) * s1
            if n == b:
                new = jnp.where(sub > r + 1, new, jnp.where(sub == r + 1, next_row, m[n]))
            m[n] = new
    return m


def factor_inverse(gram):
    tiles, rank, _ = gram.shape
    width = tiles * NB
    lane = lax.broadcasted_iota(jnp.int32, (NB, width), 1)
    row = lax.broadcasted_iota(jnp.int32, (NB, width), 0)
    within = lane & (NB - 1)
    square_row = lax.broadcasted_iota(jnp.int32, (width, width), 0)
    square_lane = lax.broadcasted_iota(jnp.int32, (width, width), 1)
    same = (square_row & -NB) == (square_lane & -NB)

    def step(n, carry):
        start = pl.multiple_of(n * NB, NB)
        stop = start + NB
        block = pl.ds(start, NB)
        rows = [gram[i, block, :] for i in range(tiles)]
        packed = jnp.zeros((NB, width), F32)
        for i in range(tiles):
            moved = pltpu.roll(rows[i], (i * NB - start) & (width - 1), 1)
            packed = jnp.where(lane - within == i * NB, moved, packed)
        m = eliminate([packed[k : k + 8] for k in range(0, NB, 8)], width)
        m = jnp.concatenate(m, axis=0)
        pivots = jnp.take_along_axis(m, lane - within + row, axis=1)
        unit = jnp.where(within == row, 1.0, jnp.where(within < row, m, 0.0)) / jnp.sqrt(pivots)
        diagonal = jnp.where(same, jnp.concatenate([unit] * tiles, axis=0), 0.0)
        lines = fine(diagonal, jnp.concatenate(rows, axis=0), 1, 0)
        inside = (lane >= start) & (lane < stop)
        for i in range(tiles):
            own = pltpu.roll(unit, (start - i * NB) & (width - 1), 1)
            line = jnp.where(inside, own, lines[i * NB : (i + 1) * NB])
            gram[i, block, :] = jnp.where(lane < stop, line, 0.0)
            rest = gram[i]
            kept = jnp.where((square_lane >= start) & (square_lane < stop), 0.0, rest)
            gram[i] = jnp.where(square_row >= stop, kept - fine(line, line, 0, 0), rest)
        return carry

    lax.fori_loop(0, rank // NB, step, 0)


def project_kernel(tiles, columns):
    def kernel(q_ref, left_hbm, coupling, tright, pivot, wide, *refs):
        line_pieces, refs = refs[:CHIPS], refs[CHIPS:]
        side_pieces, refs = refs[: len(SIDE_ORDER)], refs[len(SIDE_ORDER) :]
        exact, gram, keep, send, whole, target, share, flipped, left, done = refs
        copy = pltpu.make_async_copy(left_hbm, left, done)
        copy.start()
        q = q_ref[0]
        order = whole.shape[1]
        own = pl.ds(pl.multiple_of(q * wide.shape[1], wide.shape[1]), wide.shape[1])
        for k, piece in enumerate(line_pieces):
            put_line(q, k, 0, piece[...], whole, target, share)
        for piece, ks in zip(side_pieces, SIDE_ORDER):
            for n, k in enumerate(ks):
                put_line(q, k, 1, piece[n], whole, target, share)

        def square(i, carry):
            both = jnp.concatenate(halves(share[i]), axis=0)
            t = jnp.concatenate([target[i], target[i]], axis=1)
            t_own = jnp.concatenate([target[i, own, :], target[i, own, :]], axis=1)
            exact[i] = wide[i] + dims(t_own, both, 1, 0)
            whole[i] = (whole[i].astype(F32) + dims(t, both, 1, 0)).astype(BF)
            flipped[i] = whole[i].T
            gram[i] = dims(flipped[i], whole[i], 1, 0) * (1.0 / order)
            return carry

        lax.fori_loop(0, tiles, square, 0)
        copy.wait()
        factor_inverse(gram)

        def tile(i, carry):
            inverse = gram[i]
            both = jnp.concatenate([left[i, j] for j in range(columns)], axis=1)
            seen = dims(flipped[i], both, 1, 0)
            span = inverse.shape[1]
            mixed = [
                fine(seen[:, j * span : (j + 1) * span], coupling[i, j], 1, 0) for j in range(columns)
            ]
            mixed.append(dims(flipped[i], target[i], 1, 0))
            solved = fine(inverse, jnp.concatenate(mixed, axis=1), 1, 0).astype(BF)
            u = in_turn(q, [pivot.at[j] for j in range(columns)])
            spread(q, i, dims(u, -solved[:, : columns * span], 1, 1), keep, send)
            keep[0, i] = keep[0, i] + dims(tright[i], solved[:, columns * span :], 1, 1)
            return carry

        lax.fori_loop(0, tiles, tile, 0)

    return kernel


def vmem(n):
    return [pl.BlockSpec(memory_space=pltpu.VMEM)] * n


def basis_kernel(exact, inverse, out):
    for i in range(exact.shape[0]):
        out[:, i, :] = fine(exact[i], inverse[i], 1, 1)


def anywhere(n):
    return [pl.BlockSpec(memory_space=pl.ANY)] * n


def smem(n):
    return [pl.BlockSpec(memory_space=pltpu.SMEM)] * n


def per_device(
    left_factor, right_factor, pivot_left, pivot_right, target_left, target_right, probe, ranks
):
    tiles, columns, order, rank = left_factor.shape
    span = target_left.shape[0]
    n_col = CHIPS * CORES
    p = jnp.full((1,), lax.axis_index("prow"), jnp.int32)
    q = jnp.full((1,), lax.axis_index("pcol"), jnp.int32)
    right_first = first_stage(pivot_right, along_y)
    left_first = first_stage(jnp.concatenate([pivot_left, probe[None]]), along_x)
    right_plane = second_stage(right_first, along_x, "rights")
    left_plane = second_stage(left_first, along_y, "lefts")
    left_own = jnp.transpose(target_left, (1, 0, 2))
    right_own = jnp.transpose(target_right, (1, 0, 2))

    few = 2 * rank // n_col
    tall = (CHIPS, tiles, span + few, rank)
    coupling, keep, send, pivot = pl.pallas_call(
        sample_kernel(tiles, columns),
        out_shape=[
            jax.ShapeDtypeStruct((tiles, columns, rank, rank), F32),
            jax.ShapeDtypeStruct(tall, F32),
            jax.ShapeDtypeStruct(tall, BF),
            jax.ShapeDtypeStruct((columns, order, rank), BF),
        ],
        in_specs=smem(3) + anywhere(2) + vmem(1 + SIDE + PIECES),
        scratch_shapes=[
            pltpu.VMEM((columns, order, rank), BF),
            pltpu.VMEM((1, order, rank), BF),
            pltpu.VMEM((columns, rank, order), BF),
            pltpu.VMEM((columns, rank, rank), F32),
            pltpu.VMEM((rank, rank), F32),
            pltpu.VMEM(left_factor.shape, BF),
            pltpu.VMEM(left_factor.shape, BF),
            pltpu.SemaphoreType.DMA((2,)),
        ],
        name="sample",
    )(p, q, ranks, left_factor, right_factor, right_own, *right_plane, *left_plane)

    wide, line = pl.pallas_call(
        samples_kernel,
        out_shape=[
            jax.ShapeDtypeStruct((tiles, span, rank), F32),
            jax.ShapeDtypeStruct((tiles, 2 * span + few, rank), BF),
        ],
        name="samples_sum",
    )(*scatter_line(keep, send, F32, few // 2), left_own)

    share = (CHIPS, tiles, span, rank)
    exact, inverse, keep, send = pl.pallas_call(
        project_kernel(tiles, columns),
        out_shape=[
            jax.ShapeDtypeStruct((tiles, span, rank), F32),
            jax.ShapeDtypeStruct((tiles, rank, rank), F32),
            jax.ShapeDtypeStruct(share, F32),
            jax.ShapeDtypeStruct(share, BF),
        ],
        in_specs=smem(1) + anywhere(1) + vmem(4 + CHIPS + len(SIDE_ORDER)),
        scratch_shapes=[
            pltpu.VMEM((tiles, order, rank), BF),
            pltpu.VMEM((tiles, order, rank), BF),
            pltpu.VMEM((tiles, rank, rank), F32),
            pltpu.VMEM((tiles, rank, order), BF),
            pltpu.VMEM(left_factor.shape, BF),
            pltpu.SemaphoreType.DMA,
        ],
        name="project",
    )(q, left_factor, coupling, right_own, pivot, wide, *gather_line(line))
    basis = pl.pallas_call(
        basis_kernel, out_shape=jax.ShapeDtypeStruct((span, tiles, rank), F32), name="basis"
    )(exact, inverse)
    coefficient = pl.pallas_call(
        finish_kernel,
        out_shape=jax.ShapeDtypeStruct((span, tiles, rank), F32),
        name="finish",
    )(*scatter_line(keep, send, BF, 0))
    return (basis, coefficient)


def solution(mesh):
    in_specs = (
        P("prow", "pcol", None, None),
        P("prow", "pcol", None, None),
        P("pcol", "prow", None),
        P("pcol", "prow", None),
        P("pcol", "prow", None),
        P("pcol", "prow", None),
        P("prow", None),
        P("prow", "pcol"),
    )
    out_specs = (P("pcol", "prow", None), P("pcol", "prow", None))

    return jax.shard_map(per_device, mesh=mesh, in_specs=in_specs, out_specs=out_specs, check_vma=False)
```
